512 devices in a mesh: dp: 32 (over z, x), tensor: 16 (over y, core).
Axes of the slice: x: 4, y: 8, z: 8, core: 2. Of those that a mesh axis runs over, the one named last changes fastest.
Arguments:
- tokens: int32 [64, 4], P('dp'), may hold values from 0 to 77823
- embed_table: bfloat16 [77824, 3584], P('dp', 'tensor'), may hold values from -6 to 6
- norm_gain: bfloat16 [3584], P('tensor'), may hold values from 0.099609375 to 1.8984375
- w_query: bfloat16 [3584, 2048], P('tensor'), may hold values from -0.09375 to 0.09375
- w_key_value: bfloat16 [3584, 1024], P('tensor'), may hold values from -0.09375 to 0.09375
- cache_keys: bfloat16 [64, 4, 64, 128], P('dp'), may hold values from -6 to 6
- cache_values: bfloat16 [64, 4, 64, 128], P('dp'), may hold values from -6 to 6
- cache_len: int32 [64], P('dp'), may hold values from 1 to 64, 2048 in all
- teacher_rows: bfloat16 [512, 8192], P('dp', 'tensor'), may hold values from -6 to 6
- w_llama: bfloat16 [8192, 2, 14336], P('tensor', None, 'dp'), may hold values from -0.0625 to 0.0625
- w_qwen: bfloat16 [8192, 2, 14784], P('tensor', None, 'dp'), may hold values from -0.0625 to 0.0625
- rollout_len: int32 [32, 4], P('dp'), may hold values from 1 to 8, 16 in all within a row
- teacher_of: int32 [32, 4], P('dp'), may hold values from 0 to 1
Outputs:
- attn_out: bfloat16 [64, 4, 2048], P('dp', None, 'tensor')
- llama_hidden: bfloat16 [512, 14336], P('tensor', 'dp')
- qwen_hidden: bfloat16 [512, 14784], P('tensor', 'dp')
The draws below stay inside these ranges and needn't reach their ends.
Inputs may be any that keep to these rules, and one draw needn't show every extreme that they name: `cache_len`: at least one rollout fills all 64 slots. `rollout_len`: each row sums to 16; the longest rollout of a row has 8 token rows.
All inputs are finite; a program needn't handle non-finite values. No bound on the sum of `cache_len` on one device may be relied on, other than what follows from the above.
Results may differ from the reference program's by a relative error of at most 0.01.
Values may be sent and summed in bfloat16 or wider, within the bound.
No kernel may reach another device: no remote copies, remote signals or barrier semaphores. Data moves between devices by JAX's collectives and lax.ppermute only.
A program may use at most 64 MiB of HBM per device.

```python
import math
import jax
import jax.numpy as jnp
import numpy as np
from jax import lax

DS = 3584
HEADS = 16
KVH = 4
HD = 128
VOCAB = 77824
STEPS = 4
CACHE = 64
DT = 8192
FFL = 14336
FFQ = 14784
TT_DEV = 16
RF = 4
GROUPS = 32
BATCH = 64
ROWS = 512


def set_ends(array, key, smallest, high):
    shape = array.shape
    place = [jax.random.randint(jax.random.fold_in(key, axis), (), 0, shape[axis]) for axis in range(len(shape))]
    array = array.at[tuple(place)].set(smallest)
    longest = shape.index(max(shape))
    place[longest] = (place[longest] + 1) % shape[longest]
    return array.at[tuple(place)].set(high)


def steps_of(stream_key, extent, split, low, top_value):
    level, own = 1.0, jax.random.fold_in(stream_key, 6)
    for axis_at, shards_of in split:
        heights = jnp.exp(jax.random.uniform(jax.random.fold_in(own, axis_at), (shards_of,), jnp.float32, low / len(split), top_value / len(split)))
        level = level * jnp.repeat(heights, extent[axis_at] // shards_of).reshape([-1 if axis == axis_at else 1 for axis in range(len(extent))])
    return level


def profile(count, total, most, skew):
    portions = [(1 << 20) // math.isqrt(standing ** skew) + 1 for standing in range(2, count + 1)]
    spare, counts = total - most - (count - 1), [1] * (count - 1)
    while spare > 0:
        free = [i for i in range(count - 1) if counts[i] < most]
        pool, budget = sum([portions[i] for i in free]), spare
        for i in free:
            more = min(most - counts[i], max(1, budget * portions[i] // pool), spare)
            counts[i] = counts[i] + more
            spare = spare - more
    return np.array([most] + counts)


def uneven_parts(rng, number_of, total, bound, lean):
    if number_of == 2:
        one = jax.random.randint(rng, (), max(1, total - bound), min(bound, total - 1) + 1)
        return jnp.stack([one, total - one])
    sizes = jnp.asarray(profile(number_of, total, bound, lean), jnp.int32)
    couples = (number_of - 1) // 2
    source_of, sink = sizes[1:1 + 2 * couples:2], sizes[2:2 + 2 * couples:2]
    margin = jnp.minimum(source_of - 1, bound - sink)
    shifted = jax.random.randint(jax.random.fold_in(rng, 1), (couples,), 0, 1 << 20) % (margin + 1)
    sizes = sizes.at[1:1 + 2 * couples:2].set(source_of - shifted).at[2:2 + 2 * couples:2].set(sink + shifted)
    return sizes[jax.random.permutation(jax.random.fold_in(rng, 2), number_of)]


def scatter_about(key, shape, scale, limit, shards=(), held_as=jnp.bfloat16):
    result = scale * jax.random.normal(key, shape, jnp.float32)
    if shards:
        result = result * steps_of(key, shape, shards, -0.22, 0.18)
    return jnp.clip(result, -limit, limit).astype(held_as)


def setup_inputs(seed: int = 0) -> dict:
    arg_keys = jax.random.split(jax.random.key(seed), 14)
    return {
        "tokens": set_ends(jax.random.randint(arg_keys[0], (BATCH, STEPS), 0, VOCAB), jax.random.fold_in(arg_keys[0], 1), 0, VOCAB - 1).astype(jnp.int32),
        "embed_table": scatter_about(arg_keys[1], (VOCAB, DS), 1.0, 6.0, ((0, 32), (1, 16))),
        "norm_gain": jnp.clip(1.0 + 0.18 * jax.random.normal(arg_keys[2], (DS,), jnp.float32), 0.099609375, 1.8984375).astype(jnp.bfloat16),
        "w_query": scatter_about(arg_keys[3], (DS, HEADS * HD), DS ** -0.5, 0.09375, ((0, 16),)),
        "w_key_value": scatter_about(arg_keys[4], (DS, 2 * KVH * HD), DS ** -0.5, 0.09375, ((0, 16),)),
        "cache_keys": scatter_about(arg_keys[5], (BATCH, KVH, CACHE, HD), 1.0, 6.0, ((0, 32),)),
        "cache_values": scatter_about(arg_keys[6], (BATCH, KVH, CACHE, HD), 1.0, 6.0, ((0, 32),)),
        "cache_len": uneven_parts(arg_keys[7], BATCH, BATCH * CACHE // 2, CACHE, 2).astype(jnp.int32),
        "teacher_rows": scatter_about(arg_keys[8], (ROWS, DT), 1.0, 6.0, ((0, 32), (1, 16))),
        "w_llama": scatter_about(arg_keys[9], (DT, 2, FFL), DT ** -0.5, 0.0625, ((0, 16), (2, 32))),
        "w_qwen": scatter_about(arg_keys[10], (DT, 2, FFQ), DT ** -0.5, 0.0625, ((0, 16), (2, 32))),
        "rollout_len": jax.vmap(lambda own: uneven_parts(own, RF, TT_DEV, TT_DEV // 2, 2))(jax.random.split(arg_keys[11], GROUPS)).reshape((GROUPS, RF)).astype(jnp.int32),
        "teacher_of": set_ends(jax.random.randint(arg_keys[12], (GROUPS, RF), 0, 2), jax.random.fold_in(arg_keys[12], 1), 0, 1).astype(jnp.int32),
    }


def row_owner(rollout_len, teacher_of, per_group):
    ends = jnp.cumsum(rollout_len, axis=1)
    offset = jnp.arange(per_group, dtype=jnp.int32)
    which = lax.optimization_barrier(jnp.sum((offset[None, :, None] >= ends[:, None, :]).astype(jnp.int32), axis=2))
    slots = jnp.arange(rollout_len.shape[1], dtype=jnp.int32)
    pick = (which[:, :, None] == slots[None, None, :]).astype(jnp.int32)
    return lax.optimization_barrier(jnp.sum(pick * teacher_of[:, None, :], axis=2)).reshape(-1)

def attend(query, keys_cache, values_cache, keys_new, values_new, cache_len):
    scale = 1.0 / math.sqrt(query.shape[-1])
    query_f = query.astype(jnp.float32)
    score_cache = jnp.einsum('bshd,bhld->bshl', query_f, keys_cache.astype(jnp.float32)) * scale
    score_new = jnp.einsum('bshd,bthd->bsht', query_f, keys_new.astype(jnp.float32)) * scale
    live = jnp.arange(keys_cache.shape[2], dtype=jnp.int32)[None, :] < cache_len[:, None]
    steps = query.shape[1]
    causal = jnp.arange(steps)[:, None] >= jnp.arange(steps)[None, :]
    score_cache = jnp.where(live[:, None, None, :], score_cache, -jnp.inf)
    score_new = jnp.where(causal[None, :, None, :], score_new, -jnp.inf)
    top = jnp.maximum(lax.optimization_barrier(jnp.max(score_cache, axis=3)), lax.optimization_barrier(jnp.max(score_new, axis=3)))[..., None]
    exp_cache = jnp.exp(score_cache - top)
    exp_new = jnp.exp(score_new - top)
    total = lax.optimization_barrier(jnp.sum(exp_cache, axis=3, keepdims=True)) + lax.optimization_barrier(jnp.sum(exp_new, axis=3, keepdims=True))
    prob_cache = (exp_cache / total).astype(jnp.bfloat16)
    prob_new = (exp_new / total).astype(jnp.bfloat16)
    mixed = jnp.einsum('bshl,bhld->bshd', prob_cache.astype(jnp.float32), values_cache.astype(jnp.float32))
    mixed = mixed + jnp.einsum('bsht,bthd->bshd', prob_new.astype(jnp.float32), values_new.astype(jnp.float32))
    return mixed.astype(jnp.bfloat16)

def block_sum(rows, weights):
    return jnp.dot(rows, weights, preferred_element_type=jnp.float32)

def teacher_mlp(rows, weights, keep):
    gate = block_sum(rows, weights[:, 0, :])
    upper = block_sum(rows, weights[:, 1, :])
    return jnp.where(keep[:, None], jax.nn.silu(gate) * upper, 0.0).astype(jnp.bfloat16)

def reference(tokens, embed_table, norm_gain, w_query, w_key_value, cache_keys, cache_values, cache_len, teacher_rows, w_llama, w_qwen, rollout_len, teacher_of):
    batch = tokens.shape[0]
    embedded = jnp.take(embed_table, tokens, axis=0)
    x_float = embedded.astype(jnp.float32)
    scaled = (x_float * norm_gain.astype(jnp.float32)).astype(jnp.bfloat16).reshape(-1, DS)
    query_raw = jnp.dot(scaled, w_query, preferred_element_type=jnp.float32)
    pair_raw = jnp.dot(scaled, w_key_value, preferred_element_type=jnp.float32)
    inverse = lax.rsqrt(lax.optimization_barrier(jnp.sum(x_float * x_float, axis=2)).reshape(-1, 1) / DS + 1e-06)
    query = (query_raw * inverse).astype(jnp.bfloat16).reshape(batch, STEPS, HEADS, HD)
    key_value = (pair_raw * inverse).astype(jnp.bfloat16).reshape(batch, STEPS, 2, KVH, HD)
    kv_index = jnp.arange(HEADS, dtype=jnp.int32) // (HEADS // KVH)
    keys_cache = jnp.take(cache_keys, kv_index, axis=1)
    values_cache = jnp.take(cache_values, kv_index, axis=1)
    keys_new = jnp.take(key_value[:, :, 0], kv_index, axis=2)
    values_new = jnp.take(key_value[:, :, 1], kv_index, axis=2)
    attn_out = attend(query, keys_cache, values_cache, keys_new, values_new, cache_len).reshape(batch, STEPS, HEADS * HD)
    owner = row_owner(rollout_len, teacher_of, TT_DEV)
    llama_hidden = teacher_mlp(teacher_rows, w_llama, owner == 0)
    qwen_hidden = teacher_mlp(teacher_rows, w_qwen, owner == 1)
    return (attn_out, llama_hidden, qwen_hidden)
```

```python
import functools
import math

import jax
import jax.numpy as jnp
from jax import lax
from jax.experimental import pallas as pl
from jax.experimental.pallas import tpu as pltpu
from jax.sharding import PartitionSpec as P

DS = 3584
HD = 128
KVH = 4
EPS = 1e-06
VMEM = pltpu.MemorySpace.VMEM
SMEM = pltpu.MemorySpace.SMEM
F32 = jnp.float32
BF16 = jnp.bfloat16


def nt_dot(a, b):
    return lax.dot_general(a, b, (((1,), (1,)), ((), ())), preferred_element_type=F32)


def fetch_kernel(first_ref, ints_ref, table_ref, rows_ref, out_ref):
    groups, _, _ = ints_ref.shape
    per = out_ref.shape[1] // 2
    columns, vocab = table_ref.shape
    width = rows_ref.shape[1]
    ids = jnp.broadcast_to(ints_ref[...].astype(F32), (groups, per, ints_ref.shape[2]))
    lane = lax.broadcasted_iota(jnp.int32, ids.shape, 2)
    sub = lax.broadcasted_iota(jnp.int32, ids.shape, 1)
    ids = jnp.sum(jnp.where(lane == sub, ids, 0.0), axis=2, keepdims=True)
    ids = ids.astype(jnp.int32).reshape(groups * per, 1) - first_ref[0]
    place = lax.broadcasted_iota(jnp.int32, (groups * per, vocab), 1)
    hot = jnp.where(ids == place, 1.0, 0.0).astype(BF16)
    found = nt_dot(hot, table_ref[...]).astype(BF16).reshape(groups, per, columns)
    out_ref[:, :, :width] = jnp.broadcast_to(rows_ref[...][None], (groups,) + rows_ref.shape)
    out_ref[:, 0:per, width : width + HD] = found[:, :, :HD]
    rest = jnp.concatenate(
        [found[:, :, HD:], jnp.zeros((groups, per, 2 * HD - columns), BF16)], axis=2
    )
    out_ref[:, per:, width : width + HD] = rest


def part_kernel(
    side_ref, rows_ref, found_ref, ints_ref, gain_ref, wq_ref, wkv_ref, wl_ref, ww_ref,
    out_ref, query_ref,
):
    places, _, count, width = rows_ref.shape
    side = side_ref[0]
    per = count // 4
    columns = wq_ref.shape[0]
    half = wl_ref.shape[1]
    wide = ww_ref.shape[1]
    half_pad = (out_ref.shape[2] - HD) // 2

    rows = rows_ref[...].reshape(places * count, width)
    ints = ints_ref[...].reshape(places * 2, 1, ints_ref.shape[-1])
    lens = [ints[:, :, per + k : per + k + 1] for k in range(4)]
    kinds = [ints[:, :, per + 4 + k : per + 5 + k] for k in range(4)]
    offset = lax.broadcasted_iota(jnp.int32, (places * 2, count // 2, 1), 1)
    ends = [lens[0], lens[0] + lens[1], lens[0] + lens[1] + lens[2]]
    owner = jnp.where(
        offset < ends[0],
        kinds[0],
        jnp.where(offset < ends[1], kinds[1], jnp.where(offset < ends[2], kinds[2], kinds[3])),
    )
    first = owner.reshape(places * count, 1) == 0
    for k in range(2):
        one = nt_dot(rows, wl_ref[k])
        two = nt_dot(rows, ww_ref[k])
        one = jnp.concatenate([one, jnp.zeros((places * count, half_pad - half), F32)], axis=1)
        two = jnp.concatenate([two, jnp.zeros((places * count, half_pad - wide), F32)], axis=1)
        both = jnp.where(first, one, two).astype(BF16)
        out_ref[:, :, k * half_pad : (k + 1) * half_pad] = both.reshape(places, count, half_pad)

    embedded = jnp.sum(found_ref[...].astype(F32), axis=0)
    x = jnp.concatenate([embedded[:per], embedded[per:]], axis=1)[:, :columns]
    scaled = (x * gain_ref[...].astype(F32)).astype(BF16)
    query_ref[...] = jnp.dot(scaled, wq_ref[...], preferred_element_type=F32)
    pair = jnp.dot(scaled, wkv_ref[...], preferred_element_type=F32)
    squares = jnp.broadcast_to(jnp.sum(x * x, axis=1, keepdims=True), (per, HD))
    base = 2 * half_pad
    for p in range(places):
        start = pl.multiple_of((2 * p + side) * HD, HD)
        head = (2 * p * KVH) // (2 * places)
        key = pair[:, head * HD : (head + 1) * HD]
        value = pair[:, (KVH + head) * HD : (KVH + head + 1) * HD]
        own = query_ref[:, pl.ds(start, HD)]
        out_ref[p, :, base : base + HD] = jnp.concatenate([own, key, value, squares], axis=0).astype(BF16)


def last_kernel(
    sizes_ref, parts_ref, ints_ref, keys_ref, values_ref, attn_ref, llama_ref, qwen_ref
):
    count = parts_ref.shape[1]
    per = count // 4
    half_pad = (parts_ref.shape[2] - HD) // 2
    half = llama_ref.shape[1]
    wide = qwen_ref.shape[1]
    total = jnp.sum(parts_ref[...].astype(F32), axis=0)
    gate = total[:, :half_pad]
    up = total[:, half_pad : 2 * half_pad]
    hidden = gate / (1.0 + jnp.exp(-gate)) * up
    ints = ints_ref[...]
    lens = [ints[:, :, per + k : per + k + 1] for k in range(4)]
    kinds = [ints[:, :, per + 4 + k : per + 5 + k] for k in range(4)]
    offset = lax.broadcasted_iota(jnp.int32, (2, count // 2, 1), 1)
    ends = [lens[0], lens[0] + lens[1], lens[0] + lens[1] + lens[2]]
    owner = jnp.where(
        offset < ends[0],
        kinds[0],
        jnp.where(offset < ends[1], kinds[1], jnp.where(offset < ends[2], kinds[2], kinds[3])),
    )
    first = owner.reshape(count, 1) == 0
    llama_ref[...] = jnp.where(first, hidden, 0.0)[:, :half].astype(BF16)
    qwen_ref[...] = jnp.where(first, 0.0, hidden)[:, :wide].astype(BF16)

    student = total[:, 2 * half_pad :]
    inverse = lax.rsqrt(student[3 * per :] / DS + EPS)
    query = (student[:per] * inverse).astype(BF16)
    key = (student[per : 2 * per] * inverse).astype(BF16)
    value = (student[2 * per : 3 * per] * inverse).astype(BF16)
    rollouts, _, slots, _ = keys_ref.shape
    steps = per // rollouts
    scale = 1.0 / math.sqrt(HD)
    score_new = nt_dot(query, key) * scale
    row = lax.broadcasted_iota(jnp.int32, (per, per), 0)
    col = lax.broadcasted_iota(jnp.int32, (per, per), 1)
    fits = jnp.logical_and(row // steps == col // steps, col <= row)
    score_new = jnp.where(fits, score_new, -jnp.inf)
    for b in range(rollouts):
        score = nt_dot(query, keys_ref[b, 0]) * scale
        slot = lax.broadcasted_iota(jnp.int32, (per, slots), 1)
        score = jnp.where(slot < sizes_ref[b], score, -jnp.inf)
        mine = score_new[b * steps : (b + 1) * steps]
        score = score[b * steps : (b + 1) * steps]
        top = jnp.maximum(
            jnp.max(score, axis=1, keepdims=True), jnp.max(mine, axis=1, keepdims=True)
        )
        old_exp = jnp.exp(score - top)
        new_exp = jnp.exp(mine - top)
        whole = jnp.sum(old_exp, axis=1, keepdims=True) + jnp.sum(new_exp, axis=1, keepdims=True)
        old = (old_exp / whole).astype(BF16)
        new = (new_exp / whole).astype(BF16)
        mixed = jnp.dot(old, values_ref[b, 0], preferred_element_type=F32)
        mixed = mixed + jnp.dot(new, value, preferred_element_type=F32)
        attn_ref[b] = mixed.astype(BF16)


def whole_spec(array):
    rank = len(array.shape)
    return pl.BlockSpec(array.shape, lambda *_: (0,) * rank)


def shards(
    tokens,
    embed_table,
    norm_gain,
    w_query,
    w_key_value,
    cache_keys,
    cache_values,
    cache_len,
    teacher_rows,
    w_llama,
    w_qwen,
    rollout_len,
    teacher_of,
):
    groups = lax.axis_size("dp")
    targets = lax.axis_size("tensor")
    places = targets // 2
    dp_index = lax.axis_index("dp")
    tensor_index = lax.axis_index("tensor")
    core = tensor_index % 2
    rollouts, steps = tokens.shape
    per = rollouts * steps
    vocab, columns = embed_table.shape
    count, width = teacher_rows.shape
    rows_here = groups * count // targets

    ints = jnp.concatenate([tokens.reshape(1, per), rollout_len, teacher_of], axis=1)
    ints = jnp.broadcast_to(ints[None], (groups, 1, ints.shape[1]))
    ints = lax.all_to_all(ints, "dp", 0, 0, tiled=True)

    table = embed_table.T
    sent = pl.pallas_call(
        fetch_kernel,
        grid_spec=pltpu.PrefetchScalarGridSpec(
            num_scalar_prefetch=1,
            grid=(1,),
            in_specs=[whole_spec(ints), whole_spec(table), whole_spec(teacher_rows)],
            out_specs=pl.BlockSpec((groups, count, width + HD), lambda *_: (0, 0, 0)),
        ),
        out_shape=jax.ShapeDtypeStruct((groups, count, width + HD), BF16),
        name="fetch",
    )((dp_index * vocab).reshape(1), ints, table, teacher_rows)
    held = lax.all_to_all(sent, "dp", 0, 0, tiled=True)

    by_place = held.reshape(places, 2, rows_here, width + HD)
    ints_place = ints.reshape(places, 2, 2, 1, ints.shape[2])
    first_w = jnp.transpose(w_llama, (1, 2, 0))
    second_w = jnp.transpose(w_qwen, (1, 2, 0))
    gain = norm_gain.reshape(1, columns)
    half_pad = 512
    total_width = 2 * half_pad + HD

    def part(side):
        return pl.pallas_call(
            part_kernel,
            grid_spec=pltpu.PrefetchScalarGridSpec(
                num_scalar_prefetch=1,
                grid=(1,),
                in_specs=[
                    pl.BlockSpec((places, 1, rows_here, width), lambda i, s: (0, s[0], 0, 0)),
                    pl.BlockSpec((groups, count, HD), lambda i, s: (0, 0, width // HD)),
                    pl.BlockSpec(
                        (places, 1, 2, 1, ints.shape[2]), lambda i, s: (0, s[0], 0, 0, 0)
                    ),
                    whole_spec(gain),
                    whole_spec(w_query),
                    whole_spec(w_key_value),
                    whole_spec(first_w),
                    whole_spec(second_w),
                ],
                out_specs=pl.BlockSpec((places, rows_here, total_width), lambda *_: (0, 0, 0)),
                scratch_shapes=[pltpu.VMEM((per, w_query.shape[1]), F32)],
            ),
            out_shape=jax.ShapeDtypeStruct((places, rows_here, total_width), BF16),
            name="part",
        )(side.reshape(1), by_place, held, ints_place, gain, w_query, w_key_value, first_w, second_w)

    theirs = part(1 - core)
    theirs = lax.ppermute(theirs, "tensor", [(i, i ^ 1) for i in range(targets)])
    ours = part(core)
    joined = (theirs.astype(F32) + ours.astype(F32)).astype(BF16)
    lines = [[2 * p + c for p in range(places)] for c in range(2)]
    parts = lax.all_to_all(joined, "tensor", 0, 0, axis_index_groups=lines, tiled=True)

    kv = (tensor_index * KVH) // targets
    slots = cache_keys.shape[2]
    scalars = jnp.concatenate(
        [cache_len, jnp.stack([tensor_index, kv]).astype(jnp.int32)]
    )
    attn, llama, qwen = pl.pallas_call(
        last_kernel,
        grid_spec=pltpu.PrefetchScalarGridSpec(
            num_scalar_prefetch=1,
            grid=(1,),
            in_specs=[
                whole_spec(parts),
                pl.BlockSpec((2, 1, ints.shape[2]), lambda i, s: (s[rollouts], 0, 0)),
                pl.BlockSpec((rollouts, 1, slots, HD), lambda i, s: (0, s[rollouts + 1], 0, 0)),
                pl.BlockSpec((rollouts, 1, slots, HD), lambda i, s: (0, s[rollouts + 1], 0, 0)),
            ],
            out_specs=[
                pl.BlockSpec((rollouts, steps, HD), lambda *_: (0, 0, 0)),
                pl.BlockSpec((rows_here, w_llama.shape[2]), lambda *_: (0, 0)),
                pl.BlockSpec((rows_here, w_qwen.shape[2]), lambda *_: (0, 0)),
            ],
        ),
        out_shape=[
            jax.ShapeDtypeStruct((rollouts, steps, HD), BF16),
            jax.ShapeDtypeStruct((rows_here, w_llama.shape[2]), BF16),
            jax.ShapeDtypeStruct((rows_here, w_qwen.shape[2]), BF16),
        ],
        name="last",
    )(scalars, parts, ints, cache_keys, cache_values)
    return (attn, llama, qwen)


def solution(mesh):
    return jax.shard_map(
        shards,
        mesh=mesh,
        in_specs=(
            P("dp", None),
            P("dp", "tensor"),
            P("tensor"),
            P("tensor", None),
            P("tensor", None),
            P("dp", None, None, None),
            P("dp", None, None, None),
            P("dp"),
            P("dp", "tensor"),
            P("tensor", None, "dp"),
            P("tensor", None, "dp"),
            P("dp", None),
            P("dp", None),
        ),
        out_specs=(P("dp", None, "tensor"), P("tensor", "dp"), P("tensor", "dp")),
        check_vma=False,
    )
```

```python
import math

import jax
import jax.numpy as jnp
from jax import lax
from jax.experimental import pallas as pl
from jax.experimental.pallas import tpu as pltpu
from jax.sharding import PartitionSpec as P

DS = 3584
HD = 128
KVH = 4
EPS = 1e-06
F32 = jnp.float32
BF16 = jnp.bfloat16
VMEM_LIMIT = 28 * 2**20


def nt_dot(a, b):
    return lax.dot_general(a, b, (((1,), (1,)), ((), ())), preferred_element_type=F32)


def pack_kernel(tokens_ref, lens_ref, kinds_ref, rows_ref, out_ref):
    groups, count, _ = out_ref.shape
    width = rows_ref.shape[1]
    steps = tokens_ref.shape[1]
    lane = lax.broadcasted_iota(jnp.int32, (count, HD), 1)
    sub = lax.broadcasted_iota(jnp.int32, (count, HD), 0)
    info = jnp.zeros((count, HD), jnp.int32)
    for s in range(tokens_ref.shape[0] * steps):
        token = tokens_ref[s // steps, s % steps]
        digits = jnp.where(
            lane == 0, token >> 12, jnp.where(lane == 1, (token >> 6) & 63, token & 63)
        )
        info = jnp.where(jnp.logical_and(sub == s, lane < 3), digits, info)
    one = lens_ref[0, 0]
    two = one + lens_ref[0, 1]
    three = two + lens_ref[0, 2]
    owner = jnp.where(
        sub < one,
        kinds_ref[0, 0],
        jnp.where(sub < two, kinds_ref[0, 1], jnp.where(sub < three, kinds_ref[0, 2], kinds_ref[0, 3])),
    )
    info = jnp.where(lane == 3, owner, info).astype(F32).astype(BF16)
    out_ref[:, :, :width] = jnp.broadcast_to(rows_ref[...][None], (groups, count, width))
    out_ref[:, :, width:] = jnp.broadcast_to(info[None], (groups, count, HD))


def fetch_kernel(first_ref, info_ref, table_ref, out_ref):
    groups, per, padded = out_ref.shape
    columns, vocab = table_ref.shape
    info = info_ref[...].astype(F32)[:, :per]
    ids = info[:, :, 0:1] * 4096.0 + info[:, :, 1:2] * 64.0 + info[:, :, 2:3]
    ids = ids.astype(jnp.int32).reshape(groups * per, 1) - first_ref[0]
    place = lax.broadcasted_iota(jnp.int32, (groups * per, vocab), 1)
    hot = jnp.where(ids == place, 1.0, 0.0).astype(BF16)
    found = nt_dot(hot, table_ref[...])
    found = jnp.concatenate([found, jnp.zeros((groups * per, padded - columns), F32)], axis=1)
    out_ref[...] = found.astype(BF16).reshape(groups, per, padded)


def teacher_kernel(side_ref, rows_ref, info_ref, wl_ref, ww_ref, *rest):
    out_ref = rest[-1]
    places, _, count, width = rows_ref.shape
    half = wl_ref.shape[1]
    wide = ww_ref.shape[1]
    padded = -(-wide // HD) * HD
    rows = rows_ref[...].reshape(places * count, width)
    info = info_ref[...].astype(F32).reshape(places * count, HD)
    first = info[:, 3:4] == 0.0
    for k in range(2):
        one = nt_dot(rows, wl_ref[k])
        two = nt_dot(rows, ww_ref[k])
        one = jnp.concatenate([one, jnp.zeros((places * count, padded - half), F32)], axis=1)
        two = jnp.concatenate([two, jnp.zeros((places * count, padded - wide), F32)], axis=1)
        both = jnp.where(first, one, two).reshape(places, count, padded)
        if len(rest) > 1:
            both = both + rest[0][:, :, k * padded : (k + 1) * padded].astype(F32)
        out_ref[:, :, k * padded : (k + 1) * padded] = both.astype(BF16)


def student_kernel(side_ref, found_ref, gain_ref, wq_ref, wkv_ref, own_ref, other_ref, query_ref):
    places = own_ref.shape[0]
    per = found_ref.shape[1]
    columns = wq_ref.shape[0]
    x = jnp.sum(found_ref[...].astype(F32), axis=0)[:, :columns]
    scaled = (x * gain_ref[...].astype(F32).reshape(1, columns)).astype(BF16)
    query_ref[...] = jnp.dot(scaled, wq_ref[...], preferred_element_type=F32)
    pair = jnp.dot(scaled, wkv_ref[...], preferred_element_type=F32)
    squares = jnp.broadcast_to(jnp.sum(x * x, axis=1, keepdims=True), (per, HD))
    for out_ref, side in ((own_ref, side_ref[0]), (other_ref, 1 - side_ref[0])):
        for p in range(places):
            head = p * KVH // places
            start = pl.multiple_of((2 * p + side) * HD, HD)
            out_ref[p, :per] = query_ref[:, pl.ds(start, HD)]
            out_ref[p, per : 2 * per] = pair[:, head * HD : (head + 1) * HD]
            out_ref[p, 2 * per : 3 * per] = pair[:, (KVH + head) * HD : (KVH + head + 1) * HD]
            out_ref[p, 3 * per :] = squares


def last_kernel(
    place_ref, sizes_ref, parts_ref, info_ref, keys_ref, values_ref, attn_ref, llama_ref, qwen_ref
):
    half = llama_ref.shape[1]
    wide = qwen_ref.shape[1]
    padded = (parts_ref.shape[2] - HD) // 2
    total = jnp.sum(parts_ref[...].astype(F32), axis=0)
    gate = total[:, :padded]
    hidden = gate / (1.0 + jnp.exp(-gate)) * total[:, padded : 2 * padded]
    first = info_ref[0].astype(F32)[:, 3:4] == 0.0
    llama_ref[...] = jnp.where(first, hidden, 0.0)[:, :half].astype(BF16)
    qwen_ref[...] = jnp.where(first, 0.0, hidden)[:, :wide].astype(BF16)

    rollouts, _, slots, _ = keys_ref.shape
    per = parts_ref.shape[1] // 4
    steps = per // rollouts
    student = total[:, 2 * padded :]
    inverse = lax.rsqrt(student[3 * per :] / DS + EPS)
    query = (student[:per] * inverse).astype(BF16)
    key = (student[per : 2 * per] * inverse).astype(BF16)
    value = (student[2 * per : 3 * per] * inverse).astype(BF16)
    scale = 1.0 / math.sqrt(HD)
    score_new = nt_dot(query, key) * scale
    row = lax.broadcasted_iota(jnp.int32, (per, per), 0)
    col = lax.broadcasted_iota(jnp.int32, (per, per), 1)
    fits = jnp.logical_and(row // steps == col // steps, col <= row)
    score_new = jnp.where(fits, score_new, -jnp.inf)
    for b in range(rollouts):
        score = nt_dot(query, keys_ref[b, 0]) * scale
        slot = lax.broadcasted_iota(jnp.int32, (per, slots), 1)
        score = jnp.where(slot < sizes_ref[b], score, -jnp.inf)
        mine = score_new[b * steps : (b + 1) * steps]
        score = score[b * steps : (b + 1) * steps]
        top = jnp.maximum(
            jnp.max(score, axis=1, keepdims=True), jnp.max(mine, axis=1, keepdims=True)
        )
        old_exp = jnp.exp(score - top)
        new_exp = jnp.exp(mine - top)
        whole = jnp.sum(old_exp, axis=1, keepdims=True) + jnp.sum(new_exp, axis=1, keepdims=True)
        old = (old_exp / whole).astype(BF16)
        new = (new_exp / whole).astype(BF16)
        mixed = jnp.dot(old, values_ref[b, 0], preferred_element_type=F32)
        mixed = mixed + jnp.dot(new, value, preferred_element_type=F32)
        attn_ref[b] = mixed.astype(BF16)


def near(array):
    return pltpu.with_memory_space_constraint(array, pltpu.VMEM)


def far(array):
    return pltpu.with_memory_space_constraint(array, pltpu.HBM)


def whole_spec(array):
    rank = len(array.shape)
    return pl.BlockSpec(array.shape, lambda *_: (0,) * rank)


def call(kernel, scalars, operands, in_specs, outs, keep=True):
    return pl.pallas_call(
        kernel,
        grid_spec=pltpu.PrefetchScalarGridSpec(
            num_scalar_prefetch=len(scalars),
            grid=(1,),
            in_specs=in_specs,
            out_specs=[whole_spec(out) for out in outs],
        ),
        out_shape=[pltpu.VMEM(o.shape, o.dtype) for o in outs] if keep else outs,
        compiler_params=pltpu.CompilerParams(vmem_limit_bytes=VMEM_LIMIT),
    )(*scalars, *operands)


def shards(
    tokens,
    embed_table,
    norm_gain,
    w_query,
    w_key_value,
    cache_keys,
    cache_values,
    cache_len,
    teacher_rows,
    w_llama,
    w_qwen,
    rollout_len,
    teacher_of,
):
    groups = lax.axis_size("dp")
    targets = lax.axis_size("tensor")
    places = targets // 2
    tensor_index = lax.axis_index("tensor")
    rollouts, steps = tokens.shape
    per = rollouts * steps
    vocab, columns = embed_table.shape
    count, width = teacher_rows.shape
    rows_here = groups * count // targets
    padded = -(-columns // HD) * HD
    half_pad = -(-w_qwen.shape[2] // HD) * HD
    shape = jax.ShapeDtypeStruct
    block = width // HD

    first = (lax.axis_index("dp") * vocab).reshape(1)
    core = (tensor_index & 1).reshape(1)
    other = 1 - core
    place = jnp.stack([tensor_index, lax.div(tensor_index * KVH, targets)])

    (held,) = call(
        pack_kernel,
        [far(tokens), far(rollout_len), far(teacher_of)],
        [far(teacher_rows)],
        [whole_spec(teacher_rows)],
        [shape((groups, count, width + HD), BF16)],
    )
    held, first, core, other, place = lax.optimization_barrier((held, first, core, other, place))
    held = lax.all_to_all(held, "dp", 0, 0, tiled=True)
    held, norm_gain, cache_len, w_qwen = lax.optimization_barrier(
        (held, norm_gain, cache_len, w_qwen)
    )

    table = embed_table.T
    (found,) = call(
        fetch_kernel,
        [first],
        [near(held), near(table)],
        [
            pl.BlockSpec((groups, count, HD), lambda i, s: (0, 0, block)),
            whole_spec(table),
        ],
        [shape((groups, per, padded), BF16)],
    )
    found = lax.all_to_all(found, "dp", 0, 0, tiled=True)

    by_place = near(held.reshape(places, 2, rows_here, width + HD))
    first_w = near(jnp.transpose(w_llama, (1, 2, 0)))
    second_w = near(jnp.transpose(w_qwen, (1, 2, 0)))

    def teacher(side, extra, width_out):
        return call(
            teacher_kernel,
            [side],
            [by_place, by_place, first_w, second_w, *extra],
            [
                pl.BlockSpec((places, 1, rows_here, width), lambda i, s: (0, s[0], 0, 0)),
                pl.BlockSpec((places, 1, rows_here, HD), lambda i, s: (0, s[0], 0, block)),
                whole_spec(first_w),
                whole_spec(second_w),
                *[whole_spec(a) for a in extra],
            ],
            [shape((places, rows_here, width_out), BF16)],
        )[0]

    pairs = [(i, i ^ 1) for i in range(targets)]
    theirs = teacher(other, [], 2 * half_pad)
    theirs = lax.ppermute(theirs, "tensor", pairs)
    joined = teacher(core, [near(theirs)], 2 * half_pad + HD)

    gain = norm_gain
    found, joined, gain = lax.optimization_barrier((found, joined, gain))
    ours, theirs = pl.pallas_call(
        student_kernel,
        grid_spec=pltpu.PrefetchScalarGridSpec(
            num_scalar_prefetch=1,
            grid=(1,),
            in_specs=[whole_spec(a) for a in (found, gain, w_query, w_key_value)],
            out_specs=[pl.BlockSpec((places, 4 * per, HD), lambda *_: (0, 0, 0))] * 2,
            scratch_shapes=[pltpu.VMEM((per, w_query.shape[1]), F32)],
        ),
        out_shape=[pltpu.VMEM((places, 4 * per, HD), F32)] * 2,
        name="student",
        compiler_params=pltpu.CompilerParams(vmem_limit_bytes=VMEM_LIMIT),
    )(core, near(found), gain, far(w_query), far(w_key_value))
    theirs = lax.ppermute(theirs, "tensor", pairs)
    joined = lax.dynamic_update_slice(joined, (ours + theirs).astype(BF16), (0, 0, 2 * half_pad))

    lines = [[2 * p + c for p in range(places)] for c in range(2)]
    joined, place, cache_len = lax.optimization_barrier((joined, place, cache_len))
    parts = lax.all_to_all(joined, "tensor", 0, 0, axis_index_groups=lines, tiled=True)
    parts, place, cache_len = lax.optimization_barrier((parts, place, cache_len))

    by_target = held.reshape(targets, rows_here, width + HD)
    slots = cache_keys.shape[2]
    cache_spec = pl.BlockSpec((rollouts, 1, slots, HD), lambda i, s, _: (0, s[1], 0, 0))
    return tuple(call(
        last_kernel,
        [place, cache_len],
        [near(parts), near(by_target), cache_keys, cache_values],
        [
            whole_spec(parts),
            pl.BlockSpec((1, rows_here, HD), lambda i, s, _: (s[0], 0, block)),
            cache_spec,
            cache_spec,
        ],
        [
            shape((rollouts, steps, HD), BF16),
            shape((rows_here, w_llama.shape[2]), BF16),
            shape((rows_here, w_qwen.shape[2]), BF16),
        ],
        keep=False,
    ))


def solution(mesh):
    return jax.shard_map(
        shards,
        mesh=mesh,
        in_specs=(
            P("dp", None),
            P("dp", "tensor"),
            P("tensor"),
            P("tensor", None),
            P("tensor", None),
            P("dp", None, None, None),
            P("dp", None, None, None),
            P("dp"),
            P("dp", "tensor"),
            P("tensor", None, "dp"),
            P("tensor", None, "dp"),
            P("dp", None),
            P("dp", None),
        ),
        out_specs=(P("dp", None, "tensor"), P("tensor", "dp"), P("tensor", "dp")),
        check_vma=False,
    )
```

```python
import math

import jax
import jax.numpy as jnp
from jax import lax
from jax.experimental import pallas as pl
from jax.experimental.pallas import tpu as pltpu
from jax.sharding import PartitionSpec as P

DS = 3584
HD = 128
KVH = 4
EPS = 1e-06
F32 = jnp.float32
BF16 = jnp.bfloat16
SPARE = 48
VMEM_LIMIT = 28 * 2**20


def nt_dot(a, b):
    return lax.dot_general(a, b, (((1,), (1,)), ((), ())), preferred_element_type=F32)


def pack_kernel(tokens_ref, lens_ref, kinds_ref, rows_ref, out_ref):
    groups = out_ref.shape[0]
    count = rows_ref.shape[0]
    width = rows_ref.shape[1]
    steps = tokens_ref.shape[1]
    per = tokens_ref.shape[0] * steps
    lane = lax.broadcasted_iota(jnp.int32, (per, HD), 1)
    sub = lax.broadcasted_iota(jnp.int32, (per, HD), 0)
    info = jnp.zeros((per, HD), jnp.int32)
    for s in range(tokens_ref.shape[0] * steps):
        token = tokens_ref[s // steps, s % steps]
        digits = jnp.where(
            lane == 0, token >> 12, jnp.where(lane == 1, (token >> 6) & 63, token & 63)
        )
        info = jnp.where(jnp.logical_and(sub == s, lane < 3), digits, info)
    one = lens_ref[0, 0]
    two = one + lens_ref[0, 1]
    three = two + lens_ref[0, 2]
    for half in range(count // per):
        row = sub + half * per
        owner = jnp.where(
            row < one,
            kinds_ref[0, 0],
            jnp.where(
                row < two, kinds_ref[0, 1], jnp.where(row < three, kinds_ref[0, 2], kinds_ref[0, 3])
            ),
        )
        info = jnp.where(lane == 3 + half, owner, info)
    rows = rows_ref[...]
    for k in range(width // HD):
        piece = rows[:, k * HD : (k + 1) * HD]
        out_ref[:, k * count : (k + 1) * count] = jnp.broadcast_to(piece[None], (groups, count, HD))
    info = info.astype(F32).astype(BF16)
    out_ref[:, width // HD * count :] = jnp.broadcast_to(info[None], (groups, per, HD))


def owners(info):
    info = info.astype(F32)
    both = jnp.concatenate([info[..., 3:4], info[..., 4:5]], axis=-2)
    return both.reshape(-1, 1)


def fetch_kernel(first_ref, info_ref, table_ref, out_ref):
    groups, per, padded = out_ref.shape
    columns, vocab = table_ref.shape
    info = info_ref[...].astype(F32)
    ids = info[:, :, 0:1] * 4096.0 + info[:, :, 1:2] * 64.0 + info[:, :, 2:3]
    ids = ids.astype(jnp.int32).reshape(groups * per, 1) - first_ref[0]
    place = lax.broadcasted_iota(jnp.int32, (groups * per, vocab), 1)
    hot = jnp.where(ids == place, 1.0, 0.0).astype(BF16)
    found = nt_dot(hot, table_ref[...])
    found = jnp.concatenate([found, jnp.zeros((groups * per, padded - columns), F32)], axis=1)
    out_ref[...] = found.astype(BF16).reshape(groups, per, padded)


def teacher_kernel(side_ref, rows_ref, wl_ref, ww_ref, *rest):
    out_ref = rest[-1]
    places = rows_ref.shape[0]
    width = wl_ref.shape[2]
    count = out_ref.shape[1]
    steps = count // 2
    half = wl_ref.shape[1]
    wide = ww_ref.shape[1]
    padded = -(-wide // HD) * HD
    rows = jnp.concatenate(
        [
            rows_ref[:, 0, :, k * steps : (k + 1) * steps].reshape(places * count, HD)
            for k in range(width // HD)
        ],
        axis=1,
    )
    first = owners(rows_ref[:, 0, :, width // HD * steps :]) == 0.0
    cut = padded - HD
    for k in range(2):
        one = nt_dot(rows, wl_ref[k])
        two = nt_dot(rows, ww_ref[k])
        one = jnp.concatenate([one, jnp.zeros((places * count, padded - half), F32)], axis=1)
        two = jnp.concatenate([two, jnp.zeros((places * count, padded - wide), F32)], axis=1)
        both = jnp.where(first, one, two).reshape(places, count, padded)
        head = pl.ds(k * cut, cut)
        tail = pl.ds(2 * cut + k * HD, HD)
        main, edge = both[:, :, :cut], both[:, :, cut:]
        if len(rest) > 1:
            main = main + rest[0][:, :, head].astype(F32)
            edge = edge + rest[0][:, :, tail].astype(F32)
        out_ref[:, :, head] = main.astype(BF16)
        out_ref[:, :, tail] = edge.astype(BF16)


def student_kernel(side_ref, found_ref, gain_ref, wq_ref, wkv_ref, own_ref, other_ref, query_ref):
    places = own_ref.shape[0]
    per = found_ref.shape[1]
    columns = wq_ref.shape[0]
    x = jnp.sum(found_ref[...].astype(F32), axis=0)[:, :columns]
    scaled = (x * gain_ref[...].astype(F32).reshape(1, columns)).astype(BF16)
    query_ref[...] = jnp.dot(scaled, wq_ref[...], preferred_element_type=F32)
    pair = jnp.dot(scaled, wkv_ref[...], preferred_element_type=F32)
    squares = jnp.broadcast_to(jnp.sum(x * x, axis=1, keepdims=True), (per, HD))
    for out_ref, side in ((own_ref, side_ref[0]), (other_ref, 1 - side_ref[0])):
        for p in range(places):
            head = p * KVH // places
            start = pl.multiple_of((2 * p + side) * HD, HD)
            own = [
                query_ref[:, pl.ds(start, HD)],
                pair[:, head * HD : (head + 1) * HD],
                pair[:, (KVH + head) * HD : (KVH + head + 1) * HD],
            ]
            upper = jnp.concatenate(own, axis=0)[:, : 2 * SPARE]
            lower = jnp.concatenate([part[:, 2 * SPARE :] for part in own], axis=1)
            fill = jnp.concatenate([upper, lower], axis=0)
            pad = jnp.zeros((4 * per, HD - SPARE), F32)
            sums = jnp.concatenate([squares] * 4, axis=0)
            lane = lax.broadcasted_iota(jnp.int32, (4 * per, HD), 1)
            left = jnp.concatenate([pad, fill[:, :SPARE]], axis=1)
            out_ref[p, :, :HD] = jnp.where(lane == HD - SPARE - 1, sums, left)
            out_ref[p, :, HD:] = jnp.concatenate([pad, fill[:, SPARE:]], axis=1)


def last_kernel(
    place_ref, sizes_ref, parts_ref, info_ref, keys_ref, values_ref, attn_ref, llama_ref, qwen_ref
):
    half = llama_ref.shape[1]
    wide = qwen_ref.shape[1]
    cut = parts_ref.shape[2] // 2 - HD
    total = jnp.sum(parts_ref[...].astype(F32), axis=0)
    gate = jnp.concatenate([total[:, :cut], total[:, 2 * cut : 2 * cut + HD]], axis=1)
    up = jnp.concatenate([total[:, cut : 2 * cut], total[:, 2 * cut + HD :]], axis=1)
    gate, up = gate[:, :wide], up[:, :wide]
    hidden = gate / (1.0 + jnp.exp(-gate)) * up
    first = owners(info_ref[0]) == 0.0
    llama_ref[...] = jnp.where(first, hidden, 0.0)[:, :half].astype(BF16)
    qwen_ref[...] = jnp.where(first, 0.0, hidden)[:, :wide].astype(BF16)

    rollouts, _, slots, _ = keys_ref.shape
    per = parts_ref.shape[1] // 4
    steps = per // rollouts
    keep = HD - SPARE
    left = total[:, 2 * cut : 2 * cut + HD]
    fill = jnp.concatenate([left[:, keep:], total[:, 2 * cut + HD + keep :]], axis=1)
    rest = HD - 2 * SPARE
    student = jnp.concatenate(
        [
            jnp.concatenate(
                [fill[k * per : (k + 1) * per], fill[3 * per :, k * rest : (k + 1) * rest]], axis=1
            )
            for k in range(3)
        ],
        axis=0,
    )
    inverse = lax.rsqrt(left[:per, keep - 1 : keep] / DS + EPS)
    query = (student[:per] * inverse).astype(BF16)
    key = (student[per : 2 * per] * inverse).astype(BF16)
    value = (student[2 * per : 3 * per] * inverse).astype(BF16)
    scale = 1.0 / math.sqrt(HD)
    score_new = nt_dot(query, key) * scale
    row = lax.broadcasted_iota(jnp.int32, (per, per), 0)
    col = lax.broadcasted_iota(jnp.int32, (per, per), 1)
    fits = jnp.logical_and(row // steps == col // steps, col <= row)
    score_new = jnp.where(fits, score_new, -jnp.inf)
    for b in range(rollouts):
        score = nt_dot(query, keys_ref[b, 0]) * scale
        slot = lax.broadcasted_iota(jnp.int32, (per, slots), 1)
        score = jnp.where(slot < sizes_ref[b], score, -jnp.inf)
        mine = score_new[b * steps : (b + 1) * steps]
        score = score[b * steps : (b + 1) * steps]
        top = jnp.maximum(
            jnp.max(score, axis=1, keepdims=True), jnp.max(mine, axis=1, keepdims=True)
        )
        old_exp = jnp.exp(score - top)
        new_exp = jnp.exp(mine - top)
        whole = jnp.sum(old_exp, axis=1, keepdims=True) + jnp.sum(new_exp, axis=1, keepdims=True)
        old = (old_exp / whole).astype(BF16)
        new = (new_exp / whole).astype(BF16)
        mixed = jnp.dot(old, values_ref[b, 0], preferred_element_type=F32)
        mixed = mixed + jnp.dot(new, value, preferred_element_type=F32)
        attn_ref[b] = mixed.astype(BF16)


def near(array):
    return pltpu.with_memory_space_constraint(array, pltpu.VMEM)


def far(array):
    return pltpu.with_memory_space_constraint(array, pltpu.HBM)


def whole_spec(array):
    rank = len(array.shape)
    return pl.BlockSpec(array.shape, lambda *_: (0,) * rank)


def call(kernel, scalars, operands, in_specs, outs, keep=True):
    return pl.pallas_call(
        kernel,
        grid_spec=pltpu.PrefetchScalarGridSpec(
            num_scalar_prefetch=len(scalars),
            grid=(1,),
            in_specs=in_specs,
            out_specs=[whole_spec(out) for out in outs],
        ),
        out_shape=[pltpu.VMEM(o.shape, o.dtype) for o in outs] if keep else outs,
        compiler_params=pltpu.CompilerParams(vmem_limit_bytes=VMEM_LIMIT),
    )(*scalars, *operands)


def shards(
    tokens,
    embed_table,
    norm_gain,
    w_query,
    w_key_value,
    cache_keys,
    cache_values,
    cache_len,
    teacher_rows,
    w_llama,
    w_qwen,
    rollout_len,
    teacher_of,
):
    groups = lax.axis_size("dp")
    targets = lax.axis_size("tensor")
    places = targets // 2
    tensor_index = lax.axis_index("tensor")
    rollouts, steps = tokens.shape
    per = rollouts * steps
    vocab, columns = embed_table.shape
    count, width = teacher_rows.shape
    rows_here = groups * count // targets
    padded = -(-columns // HD) * HD
    half_pad = -(-w_qwen.shape[2] // HD) * HD
    shape = jax.ShapeDtypeStruct
    lines_held = width // HD * count + per
    block = width // HD * count // per

    first = (lax.axis_index("dp") * vocab).reshape(1)
    core = (tensor_index & 1).reshape(1)
    other = 1 - core
    place = jnp.stack([tensor_index, lax.div(tensor_index * KVH, targets)])

    (held,) = call(
        pack_kernel,
        [far(tokens), far(rollout_len), far(teacher_of)],
        [far(teacher_rows)],
        [whole_spec(teacher_rows)],
        [shape((groups, lines_held, HD), BF16)],
    )
    held, first, core, other, place = lax.optimization_barrier((held, first, core, other, place))
    held = lax.all_to_all(held, "dp", 0, 0, tiled=True)
    held, norm_gain, cache_len, w_qwen = lax.optimization_barrier(
        (held, norm_gain, cache_len, w_qwen)
    )

    table = embed_table.T
    (found,) = call(
        fetch_kernel,
        [first],
        [near(held), near(table)],
        [pl.BlockSpec((groups, per, HD), lambda i, s: (0, block, 0)), whole_spec(table)],
        [shape((groups, per, padded), BF16)],
    )
    found, w_qwen = lax.optimization_barrier((found, w_qwen))
    found = lax.all_to_all(found, "dp", 0, 0, tiled=True)

    by_place = near(held.reshape(places, 2, 2, lines_held, HD))
    first_w = near(jnp.transpose(w_llama, (1, 2, 0)))
    second_w = near(jnp.transpose(w_qwen, (1, 2, 0)))

    teacher_specs = [
        pl.BlockSpec((places, 1, 2, lines_held, HD), lambda i, s: (0, s[0], 0, 0, 0)),
        whole_spec(first_w),
        whole_spec(second_w),
    ]
    teacher_args = [by_place, first_w, second_w]
    teacher_out = shape((places, rows_here, 2 * half_pad), BF16)
    pairs = [(i, i ^ 1) for i in range(targets)]
    (theirs,) = call(teacher_kernel, [other], teacher_args, teacher_specs, [teacher_out])
    theirs = lax.ppermute(theirs, "tensor", pairs)
    (joined,) = call(
        teacher_kernel,
        [core],
        teacher_args + [near(theirs)],
        teacher_specs + [whole_spec(theirs)],
        [teacher_out],
    )

    gain = norm_gain
    found, joined, gain = lax.optimization_barrier((found, joined, gain))
    ours, theirs = pl.pallas_call(
        student_kernel,
        grid_spec=pltpu.PrefetchScalarGridSpec(
            num_scalar_prefetch=1,
            grid=(1,),
            in_specs=[whole_spec(a) for a in (found, gain, w_query, w_key_value)],
            out_specs=[pl.BlockSpec((places, 4 * per, 2 * HD), lambda *_: (0, 0, 0))] * 2,
            scratch_shapes=[pltpu.VMEM((per, w_query.shape[1]), F32)],
        ),
        out_shape=[pltpu.VMEM((places, 4 * per, 2 * HD), F32)] * 2,
        name="student",
        compiler_params=pltpu.CompilerParams(vmem_limit_bytes=VMEM_LIMIT),
    )(core, near(found), gain, near(w_query), near(w_key_value))
    theirs = lax.ppermute(theirs, "tensor", pairs)
    cut = 2 * (half_pad - HD)
    tails = joined[:, :, cut:].astype(F32) + (ours + theirs)
    joined = lax.dynamic_update_slice(joined, tails.astype(BF16), (0, 0, cut))

    lines = [[2 * p + c for p in range(places)] for c in range(2)]
    joined, place, cache_len = lax.optimization_barrier((joined, place, cache_len))
    parts = lax.all_to_all(joined, "tensor", 0, 0, axis_index_groups=lines, tiled=True)
    parts, place, cache_len = lax.optimization_barrier((parts, place, cache_len))

    by_target = held.reshape(targets, 2, lines_held, HD)
    slots = cache_keys.shape[2]
    cache_spec = pl.BlockSpec((rollouts, 1, slots, HD), lambda i, s, _: (0, s[1], 0, 0))
    return tuple(call(
        last_kernel,
        [place, cache_len],
        [near(parts), near(by_target), cache_keys, cache_values],
        [
            whole_spec(parts),
            pl.BlockSpec((1, 2, per, HD), lambda i, s, _: (s[0], 0, block, 0)),
            cache_spec,
            cache_spec,
        ],
        [
            shape((rollouts, steps, HD), BF16),
            shape((rows_here, w_llama.shape[2]), BF16),
            shape((rows_here, w_qwen.shape[2]), BF16),
        ],
        keep=False,
    ))


def solution(mesh):
    return jax.shard_map(
        shards,
        mesh=mesh,
        in_specs=(
            P("dp", None),
            P("dp", "tensor"),
            P("tensor"),
            P("tensor", None),
            P("tensor", None),
            P("dp", None, None, None),
            P("dp", None, None, None),
            P("dp"),
            P("dp", "tensor"),
            P("tensor", None, "dp"),
            P("tensor", None, "dp"),
            P("dp", None),
            P("dp", None),
        ),
        out_specs=(P("dp", None, "tensor"), P("tensor", "dp"), P("tensor", "dp")),
        check_vma=False,
    )
```

```python
import math

import jax
import jax.numpy as jnp
from jax import lax
from jax.experimental import pallas as pl
from jax.experimental.pallas import tpu as pltpu
from jax.sharding import PartitionSpec as P

DS = 3584
HD = 128
KVH = 4
EPS = 1e-06
F32 = jnp.float32
BF16 = jnp.bfloat16
SPARE = 48
VMEM_LIMIT = 16 * 2**20


def nt_dot(a, b):
    return lax.dot_general(a, b, (((1,), (1,)), ((), ())), preferred_element_type=F32)


def pack_kernel(tokens_ref, lens_ref, kinds_ref, rows_ref, out_ref):
    groups = out_ref.shape[0]
    count = rows_ref.shape[0]
    width = rows_ref.shape[1]
    steps = tokens_ref.shape[1]
    per = tokens_ref.shape[0] * steps
    lane = lax.broadcasted_iota(jnp.int32, (per, HD), 1)
    sub = lax.broadcasted_iota(jnp.int32, (per, HD), 0)
    info = jnp.zeros((per, HD), jnp.int32)
    for s in range(tokens_ref.shape[0] * steps):
        token = tokens_ref[s // steps : s // steps + 1, s % steps : s % steps + 1]
        digits = jnp.where(
            lane == 0, token >> 12, jnp.where(lane == 1, (token >> 6) & 63, token & 63)
        )
        info = jnp.where(jnp.logical_and(sub == s, lane < 3), digits, info)
    kinds = [kinds_ref[:, k : k + 1] for k in range(4)]
    one = lens_ref[:, 0:1]
    two = one + lens_ref[:, 1:2]
    three = two + lens_ref[:, 2:3]
    for half in range(count // per):
        row = sub + half * per
        owner = jnp.where(
            row < one,
            kinds[0],
            jnp.where(row < two, kinds[1], jnp.where(row < three, kinds[2], kinds[3])),
        )
        info = jnp.where(lane == 3 + half, owner, info)
    rows = rows_ref[...]
    for k in range(width // HD):
        piece = rows[:, k * HD : (k + 1) * HD]
        out_ref[:, k * count : (k + 1) * count] = jnp.broadcast_to(piece[None], (groups, count, HD))
    info = info.astype(F32).astype(BF16)
    out_ref[:, width // HD * count :] = jnp.broadcast_to(info[None], (groups, per, HD))


def owners(info):
    info = info.astype(F32)
    both = jnp.concatenate([info[..., 3:4], info[..., 4:5]], axis=-2)
    return both.reshape(-1, 1)


def fetch_kernel(first_ref, info_ref, table_ref, out_ref):
    groups, per, padded = out_ref.shape
    columns, vocab = table_ref.shape
    info = info_ref[...].astype(F32)
    ids = info[:, :, 0:1] * 4096.0 + info[:, :, 1:2] * 64.0 + info[:, :, 2:3]
    ids = ids.astype(jnp.int32).reshape(groups * per, 1) - first_ref[0]
    place = lax.broadcasted_iota(jnp.int32, (groups * per, vocab), 1)
    hot = jnp.where(ids == place, 1.0, 0.0).astype(BF16)
    found = nt_dot(hot, table_ref[...])
    found = jnp.concatenate([found, jnp.zeros((groups * per, padded - columns), F32)], axis=1)
    out_ref[...] = found.astype(BF16).reshape(groups, per, padded)


def teacher_kernel(side_ref, rows_ref, wl_ref, ww_ref, *rest):
    out_ref = rest[-1]
    places = rows_ref.shape[0]
    width = wl_ref.shape[2]
    count = out_ref.shape[1]
    steps = count // 2
    half = wl_ref.shape[1]
    wide = ww_ref.shape[1]
    padded = -(-wide // HD) * HD
    rows = jnp.concatenate(
        [
            rows_ref[:, 0, :, k * steps : (k + 1) * steps].reshape(places * count, HD)
            for k in range(width // HD)
        ],
        axis=1,
    )
    first = owners(rows_ref[:, 0, :, width // HD * steps :]) == 0.0
    cut = padded - HD
    for k in range(2):
        one = nt_dot(rows, wl_ref[k])
        two = nt_dot(rows, ww_ref[k])
        one = jnp.concatenate([one, jnp.zeros((places * count, padded - half), F32)], axis=1)
        two = jnp.concatenate([two, jnp.zeros((places * count, padded - wide), F32)], axis=1)
        both = jnp.where(first, one, two).reshape(places, count, padded)
        head = pl.ds(k * cut, cut)
        tail = pl.ds(2 * cut + k * HD, HD)
        main, edge = both[:, :, :cut], both[:, :, cut:]
        if len(rest) > 1:
            main = main + rest[0][:, :, head].astype(F32)
            edge = edge + rest[0][:, :, tail].astype(F32)
        out_ref[:, :, head] = main.astype(BF16)
        out_ref[:, :, tail] = edge.astype(BF16)


def student_kernel(side_ref, found_ref, gain_ref, wq_ref, wkv_ref, own_ref, other_ref, query_ref):
    places = own_ref.shape[0]
    per = found_ref.shape[1]
    columns = wq_ref.shape[0]
    x = jnp.sum(found_ref[...].astype(F32), axis=0)[:, :columns]
    scaled = (x * gain_ref[...].astype(F32).reshape(1, columns)).astype(BF16)
    query_ref[...] = jnp.dot(scaled, wq_ref[...], preferred_element_type=F32)
    pair = jnp.dot(scaled, wkv_ref[...], preferred_element_type=F32)
    squares = jnp.broadcast_to(jnp.sum(x * x, axis=1, keepdims=True), (per, HD))
    for out_ref, side in ((own_ref, side_ref[0]), (other_ref, 1 - side_ref[0])):
        for p in range(places):
            head = p * KVH // places
            start = pl.multiple_of((2 * p + side) * HD, HD)
            own = [
                query_ref[:, pl.ds(start, HD)],
                pair[:, head * HD : (head + 1) * HD],
                pair[:, (KVH + head) * HD : (KVH + head + 1) * HD],
            ]
            upper = jnp.concatenate(own, axis=0)[:, : 2 * SPARE]
            lower = jnp.concatenate([part[:, 2 * SPARE :] for part in own], axis=1)
            fill = jnp.concatenate([upper, lower], axis=0)
            pad = jnp.zeros((4 * per, HD - SPARE), F32)
            sums = jnp.concatenate([squares] * 4, axis=0)
            lane = lax.broadcasted_iota(jnp.int32, (4 * per, HD), 1)
            left = jnp.concatenate([pad, fill[:, :SPARE]], axis=1)
            out_ref[p, :, :HD] = jnp.where(lane == HD - SPARE - 1, sums, left)
            out_ref[p, :, HD:] = jnp.concatenate([pad, fill[:, SPARE:]], axis=1)


def last_kernel(
    place_ref, sizes_ref, parts_ref, info_ref, keys_ref, values_ref, attn_ref, llama_ref, qwen_ref
):
    half = llama_ref.shape[1]
    wide = qwen_ref.shape[1]
    cut = parts_ref.shape[2] // 2 - HD
    total = jnp.sum(parts_ref[...].astype(F32), axis=0)
    gate = jnp.concatenate([total[:, :cut], total[:, 2 * cut : 2 * cut + HD]], axis=1)
    up = jnp.concatenate([total[:, cut : 2 * cut], total[:, 2 * cut + HD :]], axis=1)
    gate, up = gate[:, :wide], up[:, :wide]
    hidden = gate / (1.0 + jnp.exp(-gate)) * up
    first = owners(info_ref[0]) == 0.0
    llama_ref[...] = jnp.where(first, hidden, 0.0)[:, :half].astype(BF16)
    qwen_ref[...] = jnp.where(first, 0.0, hidden)[:, :wide].astype(BF16)

    rollouts, _, slots, _ = keys_ref.shape
    per = parts_ref.shape[1] // 4
    steps = per // rollouts
    keep = HD - SPARE
    left = total[:, 2 * cut : 2 * cut + HD]
    fill = jnp.concatenate([left[:, keep:], total[:, 2 * cut + HD + keep :]], axis=1)
    rest = HD - 2 * SPARE
    student = jnp.concatenate(
        [
            jnp.concatenate(
                [fill[k * per : (k + 1) * per], fill[3 * per :, k * rest : (k + 1) * rest]], axis=1
            )
            for k in range(3)
        ],
        axis=0,
    )
    inverse = lax.rsqrt(left[:per, keep - 1 : keep] / DS + EPS)
    query = (student[:per] * inverse).astype(BF16)
    key = (student[per : 2 * per] * inverse).astype(BF16)
    value = (student[2 * per : 3 * per] * inverse).astype(BF16)
    scale = 1.0 / math.sqrt(HD)
    score_new = nt_dot(query, key) * scale
    row = lax.broadcasted_iota(jnp.int32, (per, per), 0)
    col = lax.broadcasted_iota(jnp.int32, (per, per), 1)
    fits = jnp.logical_and(row // steps == col // steps, col <= row)
    score_new = jnp.where(fits, score_new, -jnp.inf)
    for b in range(rollouts):
        score = nt_dot(query, keys_ref[b, 0]) * scale
        slot = lax.broadcasted_iota(jnp.int32, (per, slots), 1)
        score = jnp.where(slot < sizes_ref[b], score, -jnp.inf)
        mine = score_new[b * steps : (b + 1) * steps]
        score = score[b * steps : (b + 1) * steps]
        top = jnp.maximum(
            jnp.max(score, axis=1, keepdims=True), jnp.max(mine, axis=1, keepdims=True)
        )
        old_exp = jnp.exp(score - top)
        new_exp = jnp.exp(mine - top)
        whole = jnp.sum(old_exp, axis=1, keepdims=True) + jnp.sum(new_exp, axis=1, keepdims=True)
        old = (old_exp / whole).astype(BF16)
        new = (new_exp / whole).astype(BF16)
        mixed = jnp.dot(old, values_ref[b, 0], preferred_element_type=F32)
        mixed = mixed + jnp.dot(new, value, preferred_element_type=F32)
        attn_ref[b] = mixed.astype(BF16)


def near(array):
    return pltpu.with_memory_space_constraint(array, pltpu.VMEM)


def far(array):
    return pltpu.with_memory_space_constraint(array, pltpu.HBM)


def whole_spec(array):
    rank = len(array.shape)
    return pl.BlockSpec(array.shape, lambda *_: (0,) * rank)


def call(kernel, scalars, operands, in_specs, outs, keep=True):
    return pl.pallas_call(
        kernel,
        grid_spec=pltpu.PrefetchScalarGridSpec(
            num_scalar_prefetch=len(scalars),
            grid=(1,),
            in_specs=in_specs,
            out_specs=[whole_spec(out) for out in outs],
        ),
        out_shape=[pltpu.VMEM(o.shape, o.dtype) for o in outs] if keep else outs,
        compiler_params=pltpu.CompilerParams(vmem_limit_bytes=VMEM_LIMIT),
    )(*scalars, *operands)


def shards(
    tokens,
    embed_table,
    norm_gain,
    w_query,
    w_key_value,
    cache_keys,
    cache_values,
    cache_len,
    teacher_rows,
    w_llama,
    w_qwen,
    rollout_len,
    teacher_of,
):
    groups = lax.axis_size("dp")
    targets = lax.axis_size("tensor")
    places = targets // 2
    tensor_index = lax.axis_index("tensor")
    rollouts, steps = tokens.shape
    per = rollouts * steps
    vocab, columns = embed_table.shape
    count, width = teacher_rows.shape
    rows_here = groups * count // targets
    padded = -(-columns // HD) * HD
    half_pad = -(-w_qwen.shape[2] // HD) * HD
    shape = jax.ShapeDtypeStruct
    lines_held = width // HD * count + per
    block = width // HD * count // per

    first = (lax.axis_index("dp") * vocab).reshape(1)
    core = (tensor_index & 1).reshape(1)
    other = 1 - core
    place = jnp.stack([tensor_index, lax.div(tensor_index * KVH, targets)])

    (held,) = call(
        pack_kernel,
        [],
        [far(a) for a in (tokens, rollout_len, teacher_of, teacher_rows)],
        [whole_spec(a) for a in (tokens, rollout_len, teacher_of, teacher_rows)],
        [shape((groups, lines_held, HD), BF16)],
    )
    held, first, core, other, place = lax.optimization_barrier((held, first, core, other, place))
    held = lax.all_to_all(held, "dp", 0, 0, tiled=True)
    held, norm_gain, cache_len, w_qwen = lax.optimization_barrier(
        (held, norm_gain, cache_len, w_qwen)
    )

    table = embed_table.T
    (found,) = call(
        fetch_kernel,
        [first],
        [near(held), near(table)],
        [pl.BlockSpec((groups, per, HD), lambda i, s: (0, block, 0)), whole_spec(table)],
        [shape((groups, per, padded), BF16)],
    )
    found, w_qwen = lax.optimization_barrier((found, w_qwen))
    found = lax.all_to_all(found, "dp", 0, 0, tiled=True)

    by_place = near(held.reshape(places, 2, 2, lines_held, HD))
    first_w = near(jnp.transpose(w_llama, (1, 2, 0)))
    second_w = near(jnp.transpose(w_qwen, (1, 2, 0)))

    teacher_specs = [
        pl.BlockSpec((places, 1, 2, lines_held, HD), lambda i, s: (0, s[0], 0, 0, 0)),
        whole_spec(first_w),
        whole_spec(second_w),
    ]
    teacher_args = [by_place, first_w, second_w]
    teacher_out = shape((places, rows_here, 2 * half_pad), BF16)
    pairs = [(i, i ^ 1) for i in range(targets)]
    (theirs,) = call(teacher_kernel, [other], teacher_args, teacher_specs, [teacher_out])
    theirs = lax.ppermute(theirs, "tensor", pairs)
    (joined,) = call(
        teacher_kernel,
        [core],
        teacher_args + [near(theirs)],
        teacher_specs + [whole_spec(theirs)],
        [teacher_out],
    )
    found, joined, gain = lax.optimization_barrier((found, joined, norm_gain))
    ours, swapped = pl.pallas_call(
        student_kernel,
        grid_spec=pltpu.PrefetchScalarGridSpec(
            num_scalar_prefetch=1,
            grid=(1,),
            in_specs=[whole_spec(a) for a in (found, gain, w_query, w_key_value)],
            out_specs=[pl.BlockSpec((places, 4 * per, 2 * HD), lambda *_: (0, 0, 0))] * 2,
            scratch_shapes=[pltpu.VMEM((per, w_query.shape[1]), F32)],
        ),
        out_shape=[pltpu.VMEM((places, 4 * per, 2 * HD), F32)] * 2,
        name="student",
        compiler_params=pltpu.CompilerParams(vmem_limit_bytes=VMEM_LIMIT),
    )(core, near(found), gain, near(w_query), near(w_key_value))
    swapped = lax.ppermute(swapped, "tensor", pairs)
    cut = 2 * (half_pad - HD)
    tails = joined[:, :, cut:].astype(F32) + (ours + swapped)
    joined = lax.dynamic_update_slice(joined, tails.astype(BF16), (0, 0, cut))

    lines = [[2 * p + c for p in range(places)] for c in range(2)]
    joined, place, cache_len = lax.optimization_barrier((joined, place, cache_len))
    parts = lax.all_to_all(joined, "tensor", 0, 0, axis_index_groups=lines, tiled=True)
    parts, place, cache_len = lax.optimization_barrier((parts, place, cache_len))

    by_target = held.reshape(targets, 2, lines_held, HD)
    slots = cache_keys.shape[2]
    cache_spec = pl.BlockSpec((rollouts, 1, slots, HD), lambda i, s, _: (0, s[1], 0, 0))
    return tuple(call(
        last_kernel,
        [place, cache_len],
        [near(parts), near(by_target), cache_keys, cache_values],
        [
            whole_spec(parts),
            pl.BlockSpec((1, 2, per, HD), lambda i, s, _: (s[0], 0, block, 0)),
            cache_spec,
            cache_spec,
        ],
        [
            shape((rollouts, steps, HD), BF16),
            shape((rows_here, w_llama.shape[2]), BF16),
            shape((rows_here, w_qwen.shape[2]), BF16),
        ],
        keep=False,
    ))


def solution(mesh):
    return jax.shard_map(
        shards,
        mesh=mesh,
        in_specs=(
            P("dp", None),
            P("dp", "tensor"),
            P("tensor"),
            P("tensor", None),
            P("tensor", None),
            P("dp", None, None, None),
            P("dp", None, None, None),
            P("dp"),
            P("dp", "tensor"),
            P("tensor", None, "dp"),
            P("tensor", None, "dp"),
            P("dp", None),
            P("dp", None),
        ),
        out_specs=(P("dp", None, "tensor"), P("tensor", "dp"), P("tensor", "dp")),
        check_vma=False,
    )
```

```python
import math

import jax
import jax.numpy as jnp
from jax import lax
from jax.experimental import pallas as pl
from jax.experimental.pallas import tpu as pltpu
from jax.sharding import PartitionSpec as P

DS = 3584
HD = 128
KVH = 4
EPS = 1e-06
F32 = jnp.float32
BF16 = jnp.bfloat16
SPARE = 48
VMEM_LIMIT = 16 * 2**20


def nt_dot(a, b):
    return lax.dot_general(a, b, (((1,), (1,)), ((), ())), preferred_element_type=F32)


def pack_kernel(tokens_ref, lens_ref, kinds_ref, rows_ref, out_ref):
    groups = out_ref.shape[0]
    count = rows_ref.shape[0]
    width = rows_ref.shape[1]
    steps = tokens_ref.shape[1]
    per = tokens_ref.shape[0] * steps
    lane = lax.broadcasted_iota(jnp.int32, (per, HD), 1)
    sub = lax.broadcasted_iota(jnp.int32, (per, HD), 0)
    info = jnp.zeros((per, HD), jnp.int32)
    for s in range(tokens_ref.shape[0] * steps):
        token = tokens_ref[s // steps : s // steps + 1, s % steps : s % steps + 1]
        digits = jnp.where(
            lane == 0, token >> 12, jnp.where(lane == 1, (token >> 6) & 63, token & 63)
        )
        info = jnp.where(jnp.logical_and(sub == s, lane < 3), digits, info)
    kinds = [kinds_ref[:, k : k + 1] for k in range(4)]
    one = lens_ref[:, 0:1]
    two = one + lens_ref[:, 1:2]
    three = two + lens_ref[:, 2:3]
    for half in range(count // per):
        row = sub + half * per
        owner = jnp.where(
            row < one,
            kinds[0],
            jnp.where(row < two, kinds[1], jnp.where(row < three, kinds[2], kinds[3])),
        )
        info = jnp.where(lane == 3 + half, owner, info)
    rows = rows_ref[...]
    for k in range(width // HD):
        piece = rows[:, k * HD : (k + 1) * HD]
        out_ref[:, k * count : (k + 1) * count] = jnp.broadcast_to(piece[None], (groups, count, HD))
    info = info.astype(F32).astype(BF16)
    out_ref[:, width // HD * count :] = jnp.broadcast_to(info[None], (groups, per, HD))


def owners(info):
    info = info.astype(F32)
    both = jnp.concatenate([info[..., 3:4], info[..., 4:5]], axis=-2)
    return both.reshape(-1, 1)


def fetch_kernel(first_ref, info_ref, table_ref, out_ref):
    groups, per, columns = out_ref.shape
    vocab = table_ref.shape[1]
    info = info_ref[...].astype(F32)
    ids = info[:, :, 0:1] * 4096.0 + info[:, :, 1:2] * 64.0 + info[:, :, 2:3]
    ids = ids.astype(jnp.int32).reshape(groups * per, 1) - first_ref[0]
    place = lax.broadcasted_iota(jnp.int32, (groups * per, vocab), 1)
    hot = jnp.where(ids == place, 1.0, 0.0).astype(BF16)
    found = nt_dot(hot, table_ref[...])
    out_ref[...] = found.astype(BF16).reshape(groups, per, columns)


def teacher_kernel(side_ref, rows_ref, wl_ref, ww_ref, *rest):
    out_ref = rest[-1]
    places = rows_ref.shape[0]
    width = wl_ref.shape[2]
    count = out_ref.shape[1]
    steps = count // 2
    half = wl_ref.shape[1]
    wide = ww_ref.shape[1]
    padded = -(-wide // HD) * HD
    rows = jnp.concatenate(
        [
            rows_ref[:, 0, :, k * steps : (k + 1) * steps].reshape(places * count, HD)
            for k in range(width // HD)
        ],
        axis=1,
    )
    first = owners(rows_ref[:, 0, :, width // HD * steps :]) == 0.0
    cut = padded - HD
    for k in range(2):
        one = nt_dot(rows, wl_ref[k])
        two = nt_dot(rows, ww_ref[k])
        one = jnp.concatenate([one, jnp.zeros((places * count, padded - half), F32)], axis=1)
        two = jnp.concatenate([two, jnp.zeros((places * count, padded - wide), F32)], axis=1)
        both = jnp.where(first, one, two).reshape(places, count, padded)
        head = pl.ds(k * cut, cut)
        tail = pl.ds(2 * cut + k * HD, HD)
        main, edge = both[:, :, :cut], both[:, :, cut:]
        if len(rest) > 1:
            main = main + rest[0][:, :, head].astype(F32)
            edge = edge + rest[0][:, :, tail].astype(F32)
        out_ref[:, :, head] = main.astype(BF16)
        out_ref[:, :, tail] = edge.astype(BF16)


def student_kernel(side_ref, found_ref, gain_ref, wq_ref, wkv_ref, own_ref, other_ref, query_ref):
    places = own_ref.shape[0]
    per = found_ref.shape[1]
    columns = wq_ref.shape[0]
    x = jnp.sum(found_ref[...].astype(F32), axis=0)
    scaled = (x * gain_ref[...].astype(F32).reshape(1, columns)).astype(BF16)
    query_ref[...] = jnp.dot(scaled, wq_ref[...], preferred_element_type=F32)
    pair = jnp.dot(scaled, wkv_ref[...], preferred_element_type=F32)
    squares = jnp.broadcast_to(jnp.sum(x * x, axis=1, keepdims=True), (per, HD))
    for out_ref, side in ((own_ref, side_ref[0]), (other_ref, 1 - side_ref[0])):
        for p in range(places):
            head = p * KVH // places
            start = pl.multiple_of((2 * p + side) * HD, HD)
            own = [
                query_ref[:, pl.ds(start, HD)],
                pair[:, head * HD : (head + 1) * HD],
                pair[:, (KVH + head) * HD : (KVH + head + 1) * HD],
            ]
            upper = jnp.concatenate(own, axis=0)[:, : 2 * SPARE]
            lower = jnp.concatenate([part[:, 2 * SPARE :] for part in own], axis=1)
            fill = jnp.concatenate([upper, lower], axis=0)
            pad = jnp.zeros((4 * per, HD - SPARE), F32)
            sums = jnp.concatenate([squares] * 4, axis=0)
            lane = lax.broadcasted_iota(jnp.int32, (4 * per, HD), 1)
            left = jnp.concatenate([pad, fill[:, :SPARE]], axis=1)
            out_ref[p, :, :HD] = jnp.where(lane == HD - SPARE - 1, sums, left)
            out_ref[p, :, HD:] = jnp.concatenate([pad, fill[:, SPARE:]], axis=1)


def last_kernel(
    place_ref, sizes_ref, parts_ref, info_ref, keys_ref, values_ref, attn_ref, llama_ref, qwen_ref
):
    half = llama_ref.shape[1]
    wide = qwen_ref.shape[1]
    cut = parts_ref.shape[2] // 2 - HD
    total = jnp.sum(parts_ref[...].astype(F32), axis=0)
    gate = jnp.concatenate([total[:, :cut], total[:, 2 * cut : 2 * cut + HD]], axis=1)
    up = jnp.concatenate([total[:, cut : 2 * cut], total[:, 2 * cut + HD :]], axis=1)
    gate, up = gate[:, :wide], up[:, :wide]
    hidden = gate / (1.0 + jnp.exp(-gate)) * up
    first = owners(info_ref[0]) == 0.0
    llama_ref[...] = jnp.where(first, hidden, 0.0)[:, :half].astype(BF16)
    qwen_ref[...] = jnp.where(first, 0.0, hidden)[:, :wide].astype(BF16)

    rollouts, _, slots, _ = keys_ref.shape
    per = parts_ref.shape[1] // 4
    steps = per // rollouts
    keep = HD - SPARE
    left = total[:, 2 * cut : 2 * cut + HD]
    fill = jnp.concatenate([left[:, keep:], total[:, 2 * cut + HD + keep :]], axis=1)
    rest = HD - 2 * SPARE
    student = jnp.concatenate(
        [
            jnp.concatenate(
                [fill[k * per : (k + 1) * per], fill[3 * per :, k * rest : (k + 1) * rest]], axis=1
            )
            for k in range(3)
        ],
        axis=0,
    )
    inverse = lax.rsqrt(left[:per, keep - 1 : keep] / DS + EPS)
    query = (student[:per] * inverse).astype(BF16)
    key = (student[per : 2 * per] * inverse).astype(BF16)
    value = (student[2 * per : 3 * per] * inverse).astype(BF16)
    scale = 1.0 / math.sqrt(HD)
    score_new = nt_dot(query, key) * scale
    row = lax.broadcasted_iota(jnp.int32, (per, per), 0)
    col = lax.broadcasted_iota(jnp.int32, (per, per), 1)
    fits = jnp.logical_and(row // steps == col // steps, col <= row)
    score_new = jnp.where(fits, score_new, -jnp.inf)
    for b in range(rollouts):
        score = nt_dot(query, keys_ref[b, 0]) * scale
        slot = lax.broadcasted_iota(jnp.int32, (per, slots), 1)
        score = jnp.where(slot < sizes_ref[b], score, -jnp.inf)
        mine = score_new[b * steps : (b + 1) * steps]
        score = score[b * steps : (b + 1) * steps]
        top = jnp.maximum(
            jnp.max(score, axis=1, keepdims=True), jnp.max(mine, axis=1, keepdims=True)
        )
        old_exp = jnp.exp(score - top)
        new_exp = jnp.exp(mine - top)
        whole = jnp.sum(old_exp, axis=1, keepdims=True) + jnp.sum(new_exp, axis=1, keepdims=True)
        old = (old_exp / whole).astype(BF16)
        new = (new_exp / whole).astype(BF16)
        mixed = jnp.dot(old, values_ref[b, 0], preferred_element_type=F32)
        mixed = mixed + jnp.dot(new, value, preferred_element_type=F32)
        attn_ref[b] = mixed.astype(BF16)


def near(array):
    return pltpu.with_memory_space_constraint(array, pltpu.VMEM)


def far(array):
    return pltpu.with_memory_space_constraint(array, pltpu.HBM)


def whole_spec(array):
    rank = len(array.shape)
    return pl.BlockSpec(array.shape, lambda *_: (0,) * rank)


def call(kernel, scalars, operands, in_specs, outs, keep=True):
    return pl.pallas_call(
        kernel,
        grid_spec=pltpu.PrefetchScalarGridSpec(
            num_scalar_prefetch=len(scalars),
            grid=(1,),
            in_specs=in_specs,
            out_specs=[whole_spec(out) for out in outs],
        ),
        out_shape=[pltpu.VMEM(o.shape, o.dtype) for o in outs] if keep else outs,
        compiler_params=pltpu.CompilerParams(vmem_limit_bytes=VMEM_LIMIT),
    )(*scalars, *operands)


def shards(
    tokens,
    embed_table,
    norm_gain,
    w_query,
    w_key_value,
    cache_keys,
    cache_values,
    cache_len,
    teacher_rows,
    w_llama,
    w_qwen,
    rollout_len,
    teacher_of,
):
    groups = lax.axis_size("dp")
    targets = lax.axis_size("tensor")
    places = targets // 2
    tensor_index = lax.axis_index("tensor")
    rollouts, steps = tokens.shape
    per = rollouts * steps
    vocab, columns = embed_table.shape
    count, width = teacher_rows.shape
    rows_here = groups * count // targets
    half_pad = -(-w_qwen.shape[2] // HD) * HD
    shape = jax.ShapeDtypeStruct
    lines_held = width // HD * count + per
    block = width // HD * count // per

    first = (lax.axis_index("dp") * vocab).reshape(1)
    core = (tensor_index & 1).reshape(1)
    other = 1 - core
    place = jnp.stack([tensor_index, lax.div(tensor_index * KVH, targets)])

    (held,) = call(
        pack_kernel,
        [],
        [far(a) for a in (tokens, rollout_len, teacher_of, teacher_rows)],
        [whole_spec(a) for a in (tokens, rollout_len, teacher_of, teacher_rows)],
        [shape((groups, lines_held, HD), BF16)],
    )
    held, first, core, other, place = lax.optimization_barrier((held, first, core, other, place))
    held = lax.all_to_all(held, "dp", 0, 0, tiled=True)
    held, norm_gain, cache_len, w_qwen = lax.optimization_barrier(
        (held, norm_gain, cache_len, w_qwen)
    )

    table = embed_table.T
    (found,) = call(
        fetch_kernel,
        [first],
        [near(held), near(table)],
        [pl.BlockSpec((groups, per, HD), lambda i, s: (0, block, 0)), whole_spec(table)],
        [shape((groups, per, columns), BF16)],
    )
    found, w_qwen = lax.optimization_barrier((found, w_qwen))
    found = lax.all_to_all(found, "dp", 0, 0, tiled=True)

    by_place = near(held.reshape(places, 2, 2, lines_held, HD))
    first_w = near(jnp.transpose(w_llama, (1, 2, 0)))
    second_w = near(jnp.transpose(w_qwen, (1, 2, 0)))

    teacher_specs = [
        pl.BlockSpec((places, 1, 2, lines_held, HD), lambda i, s: (0, s[0], 0, 0, 0)),
        whole_spec(first_w),
        whole_spec(second_w),
    ]
    teacher_args = [by_place, first_w, second_w]
    teacher_out = shape((places, rows_here, 2 * half_pad), BF16)
    pairs = [(i, i ^ 1) for i in range(targets)]
    (theirs,) = call(teacher_kernel, [other], teacher_args, teacher_specs, [teacher_out])
    theirs = lax.ppermute(theirs, "tensor", pairs)
    (joined,) = call(
        teacher_kernel,
        [core],
        teacher_args + [near(theirs)],
        teacher_specs + [whole_spec(theirs)],
        [teacher_out],
    )
    found, joined, gain = lax.optimization_barrier((found, joined, norm_gain))
    ours, swapped = pl.pallas_call(
        student_kernel,
        grid_spec=pltpu.PrefetchScalarGridSpec(
            num_scalar_prefetch=1,
            grid=(1,),
            in_specs=[whole_spec(a) for a in (found, gain, w_query, w_key_value)],
            out_specs=[pl.BlockSpec((places, 4 * per, 2 * HD), lambda *_: (0, 0, 0))] * 2,
            scratch_shapes=[pltpu.VMEM((per, w_query.shape[1]), F32)],
        ),
        out_shape=[pltpu.VMEM((places, 4 * per, 2 * HD), F32)] * 2,
        name="student",
        compiler_params=pltpu.CompilerParams(vmem_limit_bytes=VMEM_LIMIT),
    )(core, near(found), gain, near(w_query), near(w_key_value))
    swapped = lax.ppermute(swapped, "tensor", pairs)
    cut = 2 * (half_pad - HD)
    tails = joined[:, :, cut:].astype(F32) + (ours + swapped)
    joined = lax.dynamic_update_slice(joined, tails.astype(BF16), (0, 0, cut))

    lines = [[2 * p + c for p in range(places)] for c in range(2)]
    joined, place, cache_len = lax.optimization_barrier((joined, place, cache_len))
    parts = lax.all_to_all(joined, "tensor", 0, 0, axis_index_groups=lines, tiled=True)
    parts, place, cache_len = lax.optimization_barrier((parts, place, cache_len))

    by_target = held.reshape(targets, 2, lines_held, HD)
    slots = cache_keys.shape[2]
    cache_spec = pl.BlockSpec((rollouts, 1, slots, HD), lambda i, s, _: (0, s[1], 0, 0))
    return tuple(call(
        last_kernel,
        [place, cache_len],
        [near(parts), near(by_target), cache_keys, cache_values],
        [
            whole_spec(parts),
            pl.BlockSpec((1, 2, per, HD), lambda i, s, _: (s[0], 0, block, 0)),
            cache_spec,
            cache_spec,
        ],
        [
            shape((rollouts, steps, HD), BF16),
            shape((rows_here, w_llama.shape[2]), BF16),
            shape((rows_here, w_qwen.shape[2]), BF16),
        ],
        keep=False,
    ))


def solution(mesh):
    return jax.shard_map(
        shards,
        mesh=mesh,
        in_specs=(
            P("dp", None),
            P("dp", "tensor"),
            P("tensor"),
            P("tensor", None),
            P("tensor", None),
            P("dp", None, None, None),
            P("dp", None, None, None),
            P("dp"),
            P("dp", "tensor"),
            P("tensor", None, "dp"),
            P("tensor", None, "dp"),
            P("dp", None),
            P("dp", None),
        ),
        out_specs=(P("dp", None, "tensor"), P("tensor", "dp"), P("tensor", "dp")),
        check_vma=False,
    )
```

```python
import math

import jax
import jax.numpy as jnp
from jax import lax
from jax.experimental import pallas as pl
from jax.experimental.pallas import tpu as pltpu
from jax.sharding import PartitionSpec as P

DS = 3584
HD = 128
KVH = 4
EPS = 1e-06
F32 = jnp.float32
BF16 = jnp.bfloat16
SPARE = 48
VMEM_LIMIT = 16 * 2**20


def nt_dot(a, b):
    return lax.dot_general(a, b, (((1,), (1,)), ((), ())), preferred_element_type=F32)


def pack_kernel(tokens_ref, lens_ref, kinds_ref, rows_ref, out_ref):
    groups = out_ref.shape[0]
    count = rows_ref.shape[0]
    width = rows_ref.shape[1]
    steps = tokens_ref.shape[1]
    per = tokens_ref.shape[0] * steps
    lane = lax.broadcasted_iota(jnp.int32, (per, HD), 1)
    sub = lax.broadcasted_iota(jnp.int32, (per, HD), 0)
    info = jnp.zeros((per, HD), jnp.int32)
    for s in range(tokens_ref.shape[0] * steps):
        token = tokens_ref[s // steps : s // steps + 1, s % steps : s % steps + 1]
        digits = jnp.where(
            lane == 0, token >> 12, jnp.where(lane == 1, (token >> 6) & 63, token & 63)
        )
        info = jnp.where(jnp.logical_and(sub == s, lane < 3), digits, info)
    kinds = [kinds_ref[:, k : k + 1] for k in range(4)]
    one = lens_ref[:, 0:1]
    two = one + lens_ref[:, 1:2]
    three = two + lens_ref[:, 2:3]
    for half in range(count // per):
        row = sub + half * per
        owner = jnp.where(
            row < one,
            kinds[0],
            jnp.where(row < two, kinds[1], jnp.where(row < three, kinds[2], kinds[3])),
        )
        info = jnp.where(lane == 3 + half, owner, info)
    rows = rows_ref[...]
    for k in range(width // HD):
        piece = rows[:, k * HD : (k + 1) * HD]
        out_ref[:, k * count : (k + 1) * count] = jnp.broadcast_to(piece[None], (groups, count, HD))
    info = info.astype(F32).astype(BF16)
    out_ref[:, width // HD * count :] = jnp.broadcast_to(info[None], (groups, per, HD))


def owners(info):
    info = info.astype(F32)
    both = jnp.concatenate([info[..., 3:4], info[..., 4:5]], axis=-2)
    return both.reshape(-1, 1)


def fetch_kernel(first_ref, info_ref, table_ref, out_ref):
    groups, per, columns = out_ref.shape
    vocab = table_ref.shape[1]
    info = info_ref[...].astype(F32)
    ids = info[:, :, 0:1] * 4096.0 + info[:, :, 1:2] * 64.0 + info[:, :, 2:3]
    ids = ids.astype(jnp.int32).reshape(groups * per, 1) - first_ref[0]
    place = lax.broadcasted_iota(jnp.int32, (groups * per, vocab), 1)
    hot = jnp.where(ids == place, 1.0, 0.0).astype(BF16)
    found = nt_dot(hot, table_ref[...])
    out_ref[...] = found.astype(BF16).reshape(groups, per, columns)


def teacher_kernel(side_ref, rows_ref, wl_ref, ww_ref, *rest):
    out_ref = rest[-1]
    places = rows_ref.shape[0]
    width = wl_ref.shape[2]
    count = out_ref.shape[1]
    steps = count // 2
    half = wl_ref.shape[1]
    wide = ww_ref.shape[1]
    padded = -(-wide // HD) * HD
    rows = jnp.concatenate(
        [
            rows_ref[:, 0, :, k * steps : (k + 1) * steps].reshape(places * count, HD)
            for k in range(width // HD)
        ],
        axis=1,
    )
    first = owners(rows_ref[:, 0, :, width // HD * steps :]) == 0.0
    cut = padded - HD
    for k in range(2):
        one = nt_dot(rows, wl_ref[k])
        two = nt_dot(rows, ww_ref[k])
        one = jnp.concatenate([one, jnp.zeros((places * count, padded - half), F32)], axis=1)
        two = jnp.concatenate([two, jnp.zeros((places * count, padded - wide), F32)], axis=1)
        both = jnp.where(first, one, two).reshape(places, count, padded)
        head = pl.ds(k * cut, cut)
        tail = pl.ds(2 * cut + k * HD, HD)
        main, edge = both[:, :, :cut], both[:, :, cut:]
        if len(rest) > 1:
            main = main + rest[0][:, :, head].astype(F32)
            edge = edge + rest[0][:, :, tail].astype(F32)
        out_ref[:, :, head] = main.astype(BF16)
        out_ref[:, :, tail] = edge.astype(BF16)


def student_kernel(side_ref, found_ref, gain_ref, wq_ref, wkv_ref, own_ref, other_ref, query_ref):
    places = own_ref.shape[0]
    per = found_ref.shape[1]
    columns = wq_ref.shape[0]
    x = jnp.sum(found_ref[...].astype(F32), axis=0)
    scaled = (x * gain_ref[...].astype(F32).reshape(1, columns)).astype(BF16)
    query_ref[...] = jnp.dot(scaled, wq_ref[...], preferred_element_type=F32)
    pair = jnp.dot(scaled, wkv_ref[...], preferred_element_type=F32)
    squares = jnp.broadcast_to(jnp.sum(x * x, axis=1, keepdims=True), (per, HD))
    for out_ref, side in ((own_ref, side_ref[0]), (other_ref, 1 - side_ref[0])):
        for p in range(places):
            head = p * KVH // places
            start = pl.multiple_of((2 * p + side) * HD, HD)
            own = [
                query_ref[:, pl.ds(start, HD)],
                pair[:, head * HD : (head + 1) * HD],
                pair[:, (KVH + head) * HD : (KVH + head + 1) * HD],
            ]
            upper = jnp.concatenate(own, axis=0)[:, : 2 * SPARE]
            lower = jnp.concatenate([part[:, 2 * SPARE :] for part in own], axis=1)
            fill = jnp.concatenate([upper, lower], axis=0)
            pad = jnp.zeros((4 * per, HD - SPARE), F32)
            sums = jnp.concatenate([squares] * 4, axis=0)
            lane = lax.broadcasted_iota(jnp.int32, (4 * per, HD), 1)
            left = jnp.concatenate([pad, fill[:, :SPARE]], axis=1)
            out_ref[p, :, :HD] = jnp.where(lane == HD - SPARE - 1, sums, left)
            out_ref[p, :, HD:] = jnp.concatenate([pad, fill[:, SPARE:]], axis=1)


def last_kernel(
    place_ref, sizes_ref, parts_ref, info_ref, keys_ref, values_ref, attn_ref, llama_ref, qwen_ref
):
    half = llama_ref.shape[1]
    wide = qwen_ref.shape[1]
    cut = parts_ref.shape[2] // 2 - HD
    total = jnp.sum(parts_ref[...].astype(F32), axis=0)
    gate = jnp.concatenate([total[:, :cut], total[:, 2 * cut : 2 * cut + HD]], axis=1)
    up = jnp.concatenate([total[:, cut : 2 * cut], total[:, 2 * cut + HD :]], axis=1)
    gate, up = gate[:, :wide], up[:, :wide]
    hidden = gate / (1.0 + jnp.exp(-gate)) * up
    first = owners(info_ref[0]) == 0.0
    llama_ref[...] = jnp.where(first, hidden, 0.0)[:, :half].astype(BF16)
    qwen_ref[...] = jnp.where(first, 0.0, hidden)[:, :wide].astype(BF16)

    rollouts, _, slots, _ = keys_ref.shape
    per = parts_ref.shape[1] // 4
    steps = per // rollouts
    keep = HD - SPARE
    left = total[:, 2 * cut : 2 * cut + HD]
    fill = jnp.concatenate([left[:, keep:], total[:, 2 * cut + HD + keep :]], axis=1)
    rest = HD - 2 * SPARE
    student = jnp.concatenate(
        [
            jnp.concatenate(
                [fill[k * per : (k + 1) * per], fill[3 * per :, k * rest : (k + 1) * rest]], axis=1
            )
            for k in range(3)
        ],
        axis=0,
    )
    inverse = lax.rsqrt(left[:per, keep - 1 : keep] / DS + EPS)
    query = (student[:per] * inverse).astype(BF16)
    key = (student[per : 2 * per] * inverse).astype(BF16)
    value = (student[2 * per : 3 * per] * inverse).astype(BF16)
    scale = 1.0 / math.sqrt(HD)
    score_new = nt_dot(query, key) * scale
    row = lax.broadcasted_iota(jnp.int32, (per, per), 0)
    col = lax.broadcasted_iota(jnp.int32, (per, per), 1)
    fits = jnp.logical_and(row // steps == col // steps, col <= row)
    score_new = jnp.where(fits, score_new, -jnp.inf)
    keys = keys_ref[:, 0].reshape(rollouts * slots, HD)
    values = values_ref[:, 0].reshape(rollouts * slots, HD)
    score = nt_dot(query, keys) * scale
    row = lax.broadcasted_iota(jnp.int32, score.shape, 0)
    slot = lax.broadcasted_iota(jnp.int32, score.shape, 1)
    live = jnp.zeros(score.shape, jnp.bool_)
    for b in range(rollouts):
        mine = jnp.logical_and(row >= b * steps, row < (b + 1) * steps)
        held = jnp.logical_and(slot >= b * slots, slot < b * slots + sizes_ref[b])
        live = jnp.logical_or(live, jnp.logical_and(mine, held))
    score = jnp.where(live, score, -jnp.inf)
    top = jnp.maximum(
        jnp.max(score, axis=1, keepdims=True), jnp.max(score_new, axis=1, keepdims=True)
    )
    old_exp = jnp.exp(score - top)
    new_exp = jnp.exp(score_new - top)
    whole = jnp.sum(old_exp, axis=1, keepdims=True) + jnp.sum(new_exp, axis=1, keepdims=True)
    old = (old_exp / whole).astype(BF16)
    new = (new_exp / whole).astype(BF16)
    mixed = jnp.dot(old, values, preferred_element_type=F32)
    mixed = mixed + jnp.dot(new, value, preferred_element_type=F32)
    for b in range(rollouts):
        attn_ref[b] = mixed[b * steps : (b + 1) * steps].astype(BF16)


def near(array):
    return pltpu.with_memory_space_constraint(array, pltpu.VMEM)


def far(array):
    return pltpu.with_memory_space_constraint(array, pltpu.HBM)


def whole_spec(array):
    rank = len(array.shape)
    return pl.BlockSpec(array.shape, lambda *_: (0,) * rank)


def call(kernel, scalars, operands, in_specs, outs, keep=True):
    return pl.pallas_call(
        kernel,
        grid_spec=pltpu.PrefetchScalarGridSpec(
            num_scalar_prefetch=len(scalars),
            grid=(1,),
            in_specs=in_specs,
            out_specs=[whole_spec(out) for out in outs],
        ),
        out_shape=[pltpu.VMEM(o.shape, o.dtype) for o in outs] if keep else outs,
        compiler_params=pltpu.CompilerParams(vmem_limit_bytes=VMEM_LIMIT),
    )(*scalars, *operands)


def shards(
    tokens,
    embed_table,
    norm_gain,
    w_query,
    w_key_value,
    cache_keys,
    cache_values,
    cache_len,
    teacher_rows,
    w_llama,
    w_qwen,
    rollout_len,
    teacher_of,
):
    groups = lax.axis_size("dp")
    targets = lax.axis_size("tensor")
    places = targets // 2
    tensor_index = lax.axis_index("tensor")
    rollouts, steps = tokens.shape
    per = rollouts * steps
    vocab, columns = embed_table.shape
    count, width = teacher_rows.shape
    rows_here = groups * count // targets
    half_pad = -(-w_qwen.shape[2] // HD) * HD
    shape = jax.ShapeDtypeStruct
    lines_held = width // HD * count + per
    block = width // HD * count // per

    first = (lax.axis_index("dp") * vocab).reshape(1)
    core = (tensor_index & 1).reshape(1)
    other = 1 - core
    place = jnp.stack([tensor_index, lax.div(tensor_index * KVH, targets)])

    (held,) = call(
        pack_kernel,
        [],
        [far(a) for a in (tokens, rollout_len, teacher_of, teacher_rows)],
        [whole_spec(a) for a in (tokens, rollout_len, teacher_of, teacher_rows)],
        [shape((groups, lines_held, HD), BF16)],
    )
    held, first, core, other, place = lax.optimization_barrier((held, first, core, other, place))
    held = lax.all_to_all(held, "dp", 0, 0, tiled=True)
    held, norm_gain, cache_len, w_qwen = lax.optimization_barrier(
        (held, norm_gain, cache_len, w_qwen)
    )

    table = embed_table.T
    (found,) = call(
        fetch_kernel,
        [first],
        [near(held), near(table)],
        [pl.BlockSpec((groups, per, HD), lambda i, s: (0, block, 0)), whole_spec(table)],
        [shape((groups, per, columns), BF16)],
    )
    found, w_qwen = lax.optimization_barrier((found, w_qwen))
    found = lax.all_to_all(found, "dp", 0, 0, tiled=True)

    by_place = near(held.reshape(places, 2, 2, lines_held, HD))
    first_w = near(jnp.transpose(w_llama, (1, 2, 0)))
    second_w = near(jnp.transpose(w_qwen, (1, 2, 0)))

    teacher_specs = [
        pl.BlockSpec((places, 1, 2, lines_held, HD), lambda i, s: (0, s[0], 0, 0, 0)),
        whole_spec(first_w),
        whole_spec(second_w),
    ]
    teacher_args = [by_place, first_w, second_w]
    teacher_out = shape((places, rows_here, 2 * half_pad), BF16)
    pairs = [(i, i ^ 1) for i in range(targets)]
    (theirs,) = call(teacher_kernel, [other], teacher_args, teacher_specs, [teacher_out])
    theirs = lax.ppermute(theirs, "tensor", pairs)
    (joined,) = call(
        teacher_kernel,
        [core],
        teacher_args + [near(theirs)],
        teacher_specs + [whole_spec(theirs)],
        [teacher_out],
    )
    found, joined, gain = lax.optimization_barrier((found, joined, norm_gain))
    ours, swapped = pl.pallas_call(
        student_kernel,
        grid_spec=pltpu.PrefetchScalarGridSpec(
            num_scalar_prefetch=1,
            grid=(1,),
            in_specs=[whole_spec(a) for a in (found, gain, w_query, w_key_value)],
            out_specs=[pl.BlockSpec((places, 4 * per, 2 * HD), lambda *_: (0, 0, 0))] * 2,
            scratch_shapes=[pltpu.VMEM((per, w_query.shape[1]), F32)],
        ),
        out_shape=[pltpu.VMEM((places, 4 * per, 2 * HD), F32)] * 2,
        name="student",
        compiler_params=pltpu.CompilerParams(vmem_limit_bytes=VMEM_LIMIT),
    )(core, near(found), gain, near(w_query), near(w_key_value))
    swapped = lax.ppermute(swapped, "tensor", pairs)
    cut = 2 * (half_pad - HD)
    tails = joined[:, :, cut:].astype(F32) + (ours + swapped)
    joined = lax.dynamic_update_slice(joined, tails.astype(BF16), (0, 0, cut))

    lines = [[2 * p + c for p in range(places)] for c in range(2)]
    joined, place, cache_len = lax.optimization_barrier((joined, place, cache_len))
    parts = lax.all_to_all(joined, "tensor", 0, 0, axis_index_groups=lines, tiled=True)
    parts, place, cache_len = lax.optimization_barrier((parts, place, cache_len))

    by_target = held.reshape(targets, 2, lines_held, HD)
    slots = cache_keys.shape[2]
    cache_spec = pl.BlockSpec((rollouts, 1, slots, HD), lambda i, s, _: (0, s[1], 0, 0))
    return tuple(call(
        last_kernel,
        [place, cache_len],
        [near(parts), near(by_target), cache_keys, cache_values],
        [
            whole_spec(parts),
            pl.BlockSpec((1, 2, per, HD), lambda i, s, _: (s[0], 0, block, 0)),
            cache_spec,
            cache_spec,
        ],
        [
            shape((rollouts, steps, HD), BF16),
            shape((rows_here, w_llama.shape[2]), BF16),
            shape((rows_here, w_qwen.shape[2]), BF16),
        ],
        keep=False,
    ))


def solution(mesh):
    return jax.shard_map(
        shards,
        mesh=mesh,
        in_specs=(
            P("dp", None),
            P("dp", "tensor"),
            P("tensor"),
            P("tensor", None),
            P("tensor", None),
            P("dp", None, None, None),
            P("dp", None, None, None),
            P("dp"),
            P("dp", "tensor"),
            P("tensor", None, "dp"),
            P("tensor", None, "dp"),
            P("dp", None),
            P("dp", None),
        ),
        out_specs=(P("dp", None, "tensor"), P("tensor", "dp"), P("tensor", "dp")),
        check_vma=False,
    )
```
